128 devices in a mesh: seq: 16 (over y, x), dp: 8 (over z, core).
Axes of the slice: x: 4, y: 4, z: 4, core: 2. Of those that a mesh axis runs over, the one named last changes fastest.
Arguments:
- queries: bfloat16 [8, 4096, 3072], P('dp', 'seq'), may hold values from -30 to 30
- keys: bfloat16 [8, 4096, 3072], P('dp', 'seq'), may hold values from -6 to 6
- values: bfloat16 [8, 4096, 3072], P('dp', 'seq'), may hold values from -6 to 6
- grad_out: bfloat16 [8, 4096, 3072], P('dp', 'seq'), may hold values from -96 to 96
- bias_table: float32 [24, 128], P('dp'), may hold values from -4 to 4
- slot_tiles: int32 [16, 5], replicated, may hold values from 0 to 31, as said below
- live: int32 [16, 7], P('seq'), may hold values from 0 to 1, as said below
- buckets: int32 [16, 7], P('seq'), may hold values from 0 to 81
Outputs:
- query_grad: bfloat16 [8, 4096, 3072], P('dp', 'seq')
- key_grad: bfloat16 [8, 4096, 3072], P('dp', 'seq')
- value_grad: bfloat16 [8, 4096, 3072], P('dp', 'seq')
- table_grad: float32 [24, 128], P('dp')
The draws below stay inside these ranges and needn't reach their ends.
Inputs may be any that keep to these rules, and one draw needn't show every extreme that they name: Entry s of row i names a key tile of query tile i - 1, i + 1, i - 2, i + 2 for s = 0, 1, 2, 3 and of query tile (i + 8) mod 16 for s = 4, that is, slot_tiles[i, s] // 2 is that query tile; where that query tile would lie outside 0 to 15 the entry names one of query tile i's own key tiles and is not live. `live`: entry 0 of every row is 1. Row 8 is 1 everywhere. Row 0 is 1 everywhere except entries 2 and 4.
All inputs are finite; a program needn't handle non-finite values.
Results may differ from the reference program's by a relative error of at most 0.008.
Values may be sent and summed in bfloat16 or wider, within the bound.
A program may use at most 192 MiB of HBM per device.

```python
import jax
import jax.numpy as jnp
from jax import lax

HEADS = 24
HEAD_DIM = 128
TOK_DEV = 256
TILE = 128
TILE_COLS = 16
SLOTS = 5
BUCKETS = 82
WIDTH = 3072
TILES_DEV = 2
QUERY_TILES = 16
KEY_TILES = 32
LENGTH = 4096
WINDOWS = 8
TABLE = 128


def draw_pattern(key):
    index = jnp.arange(QUERY_TILES, dtype=jnp.int32)[:, None]
    near = index + jnp.array([-1, 1, -2, 2], jnp.int32)[None, :]
    near_valid = (near >= 0) & (near < QUERY_TILES)
    far = (index + QUERY_TILES // 2) % QUERY_TILES
    partner = jnp.concatenate([jnp.where(near_valid, near, index), far], axis=1)
    valid = jnp.concatenate([near_valid, jnp.ones((QUERY_TILES, 1), dtype=bool)], axis=1)
    sub_tile = jax.random.randint(jax.random.fold_in(key, 11), (QUERY_TILES, SLOTS), 0, TILES_DEV)
    tiles = partner * TILES_DEV + sub_tile
    level = jax.random.randint(jax.random.fold_in(key, 12), (QUERY_TILES, 1), 0, 3)
    level = jnp.where((index == QUERY_TILES // 2) | (index == 0), 2, level)
    own_roll = jax.random.randint(jax.random.fold_in(key, 13), (QUERY_TILES, TILES_DEV), 0, 4)
    own_limit = jnp.where(level == 0, 1, jnp.where(level == 1, 2, 4))
    own_live = (own_roll < own_limit) | (jnp.arange(TILES_DEV, dtype=jnp.int32)[None, :] == 0)
    slot_roll = jax.random.randint(jax.random.fold_in(key, 14), (QUERY_TILES, SLOTS), 0, 4)
    slot_limit = jnp.where(level == 0, 0, jnp.where(level == 1, 2, 4))
    slot_live = (slot_roll < slot_limit) & valid
    live_table = jnp.concatenate([own_live, slot_live], axis=1).astype(jnp.int32)
    return (tiles.astype(jnp.int32), live_table)


def draw_slot_tiles(key, part):
    return draw_pattern(key)[0]


def draw_live(key, part):
    return draw_pattern(key)[1]


def draw_query_key(key):
    shape = (WINDOWS, LENGTH, WIDTH)
    seed_query = jax.random.fold_in(key, 21)
    seed_key = jax.random.fold_in(key, 22)
    query_value = jax.random.truncated_normal(seed_query, -6.0, 6.0, shape, jnp.float32)
    key_value = jax.random.truncated_normal(seed_key, -6.0, 6.0, shape, jnp.float32)
    return (query_value, key_value)


def draw_queries(key, part):
    return draw_query_key(key)[0].astype(jnp.bfloat16)


def draw_keys(key, part):
    return draw_query_key(key)[1].astype(jnp.bfloat16)


def touch_ends(drawn, own_key, least, high):
    index_at = [jax.random.randint(jax.random.fold_in(own_key, axis), (), 0, length) for axis, length in enumerate(drawn.shape)]
    longest = drawn.shape.index(max(drawn.shape))
    neighbour = index_at[:longest] + [(index_at[longest] + 1) % drawn.shape[longest]] + index_at[longest + 1:]
    return drawn.at[tuple(index_at)].set(least).at[tuple(neighbour)].set(high)


def levels(stream_key, extent, split, low, top_value):
    level = 1.0
    for position, shards_of in split:
        heights = jax.random.uniform(jax.random.fold_in(jax.random.fold_in(stream_key, 6), position), (shards_of,), jnp.float32, low / len(split), top_value / len(split))
        level = level * jnp.repeat(jnp.exp(heights), extent[position] // shards_of).reshape((-1,) + (1,) * (len(extent) - 1 - position))
    return level


def normal_values(stream_key, shape, width, limit, cuts=(), kind=jnp.bfloat16):
    values = jax.random.normal(stream_key, shape, jnp.float32) * width
    if len(cuts) > 0:
        values = levels(stream_key, shape, cuts, -0.22, 0.18) * values
    return jnp.clip(values, min=-limit, max=limit).astype(kind)


def setup_inputs(seed: int = 0) -> dict:
    arg_keys = jax.random.split(jax.random.key(seed), 9)
    queries = draw_queries(jax.random.fold_in(arg_keys[8], 71), 0)
    keys = draw_keys(jax.random.fold_in(arg_keys[8], 71), 0)
    values = normal_values(arg_keys[2], (WINDOWS, LENGTH, WIDTH), 1.0, 6.0, ((0, 8), (1, 16)))
    grad_out = normal_values(arg_keys[3], (WINDOWS, LENGTH, WIDTH), 16.0, 96.0, ((0, 8), (1, 16)))
    bias_table = normal_values(arg_keys[4], (HEADS, TABLE), 1.0, 4.0, ((0, 8),), jnp.float32)
    slot_tiles = draw_slot_tiles(jax.random.fold_in(arg_keys[8], 71), 0)
    live = draw_live(jax.random.fold_in(arg_keys[8], 71), 0)
    buckets = touch_ends(jax.random.randint(arg_keys[7], (QUERY_TILES, TILES_DEV + SLOTS), 0, BUCKETS), jax.random.fold_in(arg_keys[7], 1), 0, BUCKETS - 1).astype(jnp.int32)
    return dict(queries=queries, keys=keys, values=values, grad_out=grad_out, bias_table=bias_table, slot_tiles=slot_tiles, live=live, buckets=buckets)


NEGATIVE = -1e30


def rounded(array):
    low = array.astype(jnp.bfloat16)
    low = lax.optimization_barrier(low)
    return low.astype(jnp.float32)


def offset_indices():
    tile_rows = TILE // TILE_COLS
    query_pos = jnp.arange(TOK_DEV, dtype=jnp.int32)[:, None]
    key_pos = jnp.arange(TILE, dtype=jnp.int32)[None, :]
    column_index = key_pos % TILE_COLS - query_pos % TILE_COLS + TILE_COLS - 1
    row_index = key_pos // TILE_COLS - (query_pos // TILE_COLS) % tile_rows + tile_rows - 1
    return column_index, row_index


def reference(queries, keys, values, grad_out, bias_table, slot_tiles, live, buckets):
    scale = HEAD_DIM ** -0.5
    set_size = TILES_DEV + SLOTS
    column_width = 2 * TILE_COLS - 1
    row_width = 2 * (TILE // TILE_COLS) - 1
    column_index, row_index = offset_indices()
    column_table = bias_table[:, BUCKETS:BUCKETS + column_width]
    row_table = bias_table[:, BUCKETS + column_width:]
    fine_bias = column_table[:, column_index] + row_table[:, row_index]
    own_range = jnp.arange(TILES_DEV, dtype=jnp.int32)
    remote_flag = (jnp.arange(set_size, dtype=jnp.int32) >= TILES_DEV)[:, None, None]

    def one_window(arrays):
        query_all, key_all, value_all, upstream_all = arrays
        key_tiles = key_all.reshape(KEY_TILES, TILE, WIDTH)
        value_tiles = value_all.reshape(KEY_TILES, TILE, WIDTH)

        def one_tile(carry, index):
            key_grad, value_grad, table_grad = carry
            chosen = jnp.concatenate([index * TILES_DEV + own_range, slot_tiles[index].astype(jnp.int32)]).astype(jnp.int32)
            alive = live[index] > 0
            bucket_row = buckets[index].astype(jnp.int32)
            start = (index * TOK_DEV).astype(jnp.int32)
            query_block = lax.dynamic_slice_in_dim(query_all, start, TOK_DEV, 0).astype(jnp.float32).reshape(TOK_DEV, HEADS, HEAD_DIM)
            upstream = lax.dynamic_slice_in_dim(upstream_all, start, TOK_DEV, 0).astype(jnp.float32).reshape(TOK_DEV, HEADS, HEAD_DIM)
            key_set = key_tiles[chosen].astype(jnp.float32).reshape(set_size, TILE, HEADS, HEAD_DIM)
            value_set = value_tiles[chosen].astype(jnp.float32).reshape(set_size, TILE, HEADS, HEAD_DIM)
            coarse = bias_table[:, bucket_row]
            scores = jnp.einsum("qhd,skhd->hqsk", query_block, key_set) * scale
            scores = scores + coarse[:, None, :, None] + fine_bias[:, :, None, :]
            mask = alive[None, None, :, None]
            masked = jnp.where(mask, scores, NEGATIVE)
            top = jnp.max(masked, axis=(2, 3), keepdims=True)
            total = jnp.sum(jnp.where(mask, jnp.exp(masked - top), 0.0), axis=(2, 3), keepdims=True)
            log_total = top + jnp.log(total)
            attend = jnp.where(mask, jnp.exp(scores - log_total), 0.0)
            attend_grad = jnp.einsum("qhd,skhd->hqsk", upstream, value_set)
            delta = jnp.sum(attend * attend_grad, axis=(2, 3), keepdims=True)
            score_grad = attend * (attend_grad - delta)
            attend_low = rounded(attend)
            grad_low = rounded(score_grad)
            value_part = jnp.einsum("hqsk,qhd->skhd", attend_low, upstream).reshape(set_size, TILE, WIDTH)
            key_part = (jnp.einsum("hqsk,qhd->skhd", grad_low, query_block) * scale).reshape(set_size, TILE, WIDTH)
            value_part = jnp.where(remote_flag, rounded(value_part), value_part)
            key_part = jnp.where(remote_flag, rounded(key_part), key_part)
            query_grad = jnp.einsum("hqsk,skhd->qhd", grad_low, key_set) * scale
            block_sums = jnp.sum(score_grad, axis=(1, 3))
            fine_sum = jnp.sum(score_grad, axis=2)
            coarse_grad = jnp.zeros((HEADS, BUCKETS), jnp.float32).at[:, bucket_row].add(block_sums)
            column_grad = jnp.zeros((HEADS, column_width), jnp.float32).at[:, column_index].add(fine_sum)
            row_grad = jnp.zeros((HEADS, row_width), jnp.float32).at[:, row_index].add(fine_sum)
            table_grad = table_grad + jnp.concatenate([coarse_grad, column_grad, row_grad], axis=1)
            key_grad = key_grad.at[chosen].add(key_part)
            value_grad = value_grad.at[chosen].add(value_part)
            return (key_grad, value_grad, table_grad), query_grad.reshape(TOK_DEV, WIDTH).astype(jnp.bfloat16)

        start_state = (jnp.zeros((KEY_TILES, TILE, WIDTH), jnp.float32), jnp.zeros((KEY_TILES, TILE, WIDTH), jnp.float32), jnp.zeros((HEADS, TABLE), jnp.float32))
        final_state, query_rows = lax.scan(one_tile, start_state, jnp.arange(QUERY_TILES, dtype=jnp.int32))
        key_grad, value_grad, table_grad = final_state
        return (query_rows.reshape(LENGTH, WIDTH), key_grad.reshape(LENGTH, WIDTH).astype(jnp.bfloat16), value_grad.reshape(LENGTH, WIDTH).astype(jnp.bfloat16), table_grad)

    query_grad, key_grad, value_grad, table_grads = lax.map(one_window, (queries, keys, values, grad_out))
    return query_grad, key_grad, value_grad, jnp.sum(table_grads, axis=0)
```

```python
import jax
import jax.numpy as jnp
from jax import lax
from jax.experimental import pallas as pl
from jax.experimental.pallas import tpu as pltpu
from jax.sharding import PartitionSpec as P

HEADS = 24
HEAD_DIM = 128
TOK_DEV = 256
TILE = 128
TILE_COLS = 16
TILE_ROWS = TILE // TILE_COLS
SLOTS = 5
BUCKETS = 82
WIDTH = 3072
TILES_DEV = 2
ENTRIES = TILES_DEV + SLOTS
COLUMN_WIDTH = 2 * TILE_COLS - 1
TABLE = 128

SIDE = 4
SEQ = SIDE * SIDE
DP = 8
CHUNKS = HEADS // SIDE
NEGATIVE = -1e30
SCALE = HEAD_DIM ** (-0.5)
NEAR_OFFSETS = (-1, 1, -2, 2)
HIGHEST = lax.Precision.HIGHEST
MESH = pl.DeviceIdType.MESH

FROM_BELOW = tuple((q, s, q + o + SIDE) for q in range(SIDE) for s, o in enumerate(NEAR_OFFSETS) if q + o < 0)
FROM_ABOVE = tuple((q, s, q + o - SIDE) for q in range(SIDE) for s, o in enumerate(NEAR_OFFSETS) if q + o >= SIDE)
FROM_HALF = tuple((q, SLOTS - 1, q) for q in range(SIDE))
GROUPS = ((FROM_BELOW, 1), (FROM_ABOVE, SIDE - 1), (FROM_HALF, SIDE // 2))
LOCAL = tuple(
    (q, s, q + o) for q in range(SIDE) for s, o in enumerate(NEAR_OFFSETS) if 0 <= q + o < SIDE
)


def iota(shape, axis):
    return lax.broadcasted_iota(jnp.int32, shape, axis)


def kernel(
    queries, keys, values, upstream, table, slots, live, buckets,
    query_out, key_out, value_out, table_out,
    kv_in, qd_in, give0, give1, give2, got0, got1, got2, back0, back1, back2, home0, home1, home2,
    ret, acc, key_set, value_set, key_part, value_part,
    tables, entries, shifted, fine, fine_sum, coarse_sum, grads, grads_dp, grads_seq,
    kv_send, kv_recv, qd_send, qd_recv, give_send, got_recv, back_send, home_recv, ret_send, out_recv,
    table_send, table_recv, entry_send, entry_recv, dp_send, dp_recv, seq_send, seq_recv,
):
    gives, gots = (give0, give1, give2), (got0, got1, got2)
    backs, homes = (back0, back1, back2), (home0, home1, home2)
    outs = (query_out, key_out, value_out)
    place = lax.axis_index("seq")
    part = lax.axis_index("dp")
    x, y = lax.rem(place, SIDE), lax.div(place, SIDE)

    def seq_at(column, row):
        return {"seq": lax.rem(row, SIDE) * SIDE + lax.rem(column, SIDE)}

    def remote(source, target, send, recv, device):
        return pltpu.make_async_remote_copy(
            src_ref=source, dst_ref=target, send_sem=send, recv_sem=recv,
            device_id=device, device_id_type=MESH,
        )

    def arrived(buffer, semaphore):
        pltpu.make_async_copy(buffer, buffer, semaphore).wait()

    def head_columns(head):
        return pl.ds(pl.multiple_of(head * HEAD_DIM, HEAD_DIM), HEAD_DIM)

    barrier = pltpu.get_barrier_semaphore()
    for j in range(1, SEQ):
        pl.semaphore_signal(
            barrier, inc=1, device_id={"seq": lax.rem(place + j, SEQ)}, device_id_type=MESH
        )
    for j in range(1, DP):
        pl.semaphore_signal(
            barrier, inc=1, device_id={"dp": lax.rem(part + j, DP)}, device_id_type=MESH
        )

    lane = iota((8, TABLE), 1)
    row = iota((8, TABLE), 0)
    tables[part] = jnp.zeros((8, TABLE), jnp.float32)
    tables[part, 0 : HEADS // DP, :] = table[...]
    bucket = jnp.full((8, TABLE), -1, jnp.int32)
    alive = jnp.zeros((8, TABLE), jnp.int32)
    for e in range(ENTRIES):
        bucket = jnp.where(row == e, buckets[0, e], bucket)
        alive = jnp.where(row == e, live[0, e], alive)
    entries[x, 0] = (lane == bucket).astype(jnp.float32)
    entries[x, 1] = jnp.where(alive > 0, 0.0, NEGATIVE)
    grads[...] = jnp.zeros_like(grads)

    pl.semaphore_wait(barrier, SEQ - 1 + DP - 1)

    def table_copy(j):
        return remote(
            tables.at[part], tables.at[part], table_send.at[j], table_recv.at[part],
            {"dp": lax.rem(part + j, DP)},
        )

    def entry_copy(j):
        return remote(
            entries.at[x], entries.at[x], entry_send.at[j], entry_recv.at[x], seq_at(x + j, y)
        )

    def in_copies(refs, buffer, send, recv, c):
        copies = []
        for a, ref in enumerate(refs):
            for j in range(1, SIDE):
                to = lax.rem(x + j, SIDE)
                copies.append(
                    remote(
                        ref.at[:, head_columns(to * CHUNKS + c)], buffer.at[c, a, x],
                        send.at[c, a, j], recv.at[c], seq_at(to, y),
                    )
                )
        return copies

    def fetch(refs, buffer, send, recv, c):
        for copy in in_copies(refs, buffer, send, recv, c):
            copy.start()
        for a, ref in enumerate(refs):
            pltpu.make_async_copy(
                ref.at[:, head_columns(x * CHUNKS + c)], buffer.at[c, a, x], recv.at[c]
            ).start()

    kv = ((keys, values), kv_in, kv_send, kv_recv)
    qd = ((queries, upstream), qd_in, qd_send, qd_recv)

    def give_copy(g, c):
        return remote(
            gives[g].at[c], gots[g].at[c], give_send.at[c, g], got_recv.at[c, g],
            seq_at(x, y + GROUPS[g][1]),
        )

    def back_copy(g, c):
        return remote(
            backs[g].at[c], homes[g].at[c], back_send.at[c, g], home_recv.at[c, g],
            seq_at(x, y + SIDE - GROUPS[g][1]),
        )

    def ret_copies(a, c):
        return [
            remote(
                ret.at[c, a, lax.rem(x + j, SIDE)], outs[a].at[:, head_columns(x * CHUNKS + c)],
                ret_send.at[c, a, j], out_recv.at[a], seq_at(x + j, y),
            )
            for j in range(1, SIDE)
        ]

    def give_back(a, c):
        for copy in ret_copies(a, c):
            copy.start()
        pltpu.make_async_copy(
            ret.at[c, a, x], outs[a].at[:, head_columns(x * CHUNKS + c)], out_recv.at[a]
        ).start()

    def upper(query_row, q, s):
        return lax.rem(slots[lax.rem(query_row, SIDE) * SIDE + q, s], TILES_DEV) == 1

    for j in range(1, DP):
        table_copy(j).start()
    for j in range(1, SIDE):
        entry_copy(j).start()
    fetch(*kv, 0)
    fetch(*qd, 0)
    fetch(*kv, 1)
    for j in range(1, DP):
        source = lax.rem(part + j, DP)
        arrived(tables.at[source], table_recv.at[source])
    for j in range(1, SIDE):
        source = lax.rem(x + j, SIDE)
        arrived(entries.at[source], entry_recv.at[source])

    def halves(c, a, tile):
        return kv_in[c, a, tile, 0:TILE, :], kv_in[c, a, tile, TILE : 2 * TILE, :]

    def send_tiles(c):
        arrived(kv_in.at[c], kv_recv.at[c])

        @pl.when(c + 1 < CHUNKS)
        def _():
            fetch(*qd, c + 1)

        @pl.when(c + 2 < CHUNKS)
        def _():
            fetch(*kv, c + 2)

        for g, (group, distance) in enumerate(GROUPS):
            for n, (q, s, tile) in enumerate(group):
                pick = upper(y + distance, q, s)
                for a in range(2):
                    low, high = halves(c, a, tile)
                    gives[g][c, a, n] = jnp.where(pick, high, low)
            give_copy(g, c).start()

    def compute(c):
        arrived(qd_in.at[c], qd_recv.at[c])
        for g in range(3):
            arrived(gots[g].at[c], got_recv.at[c, g])
        sets = (key_set, value_set)
        for a in range(2):
            for q in range(SIDE):
                sets[a][q, 0 : 2 * TILE, :] = kv_in[c, a, q]
            for q, s, tile in LOCAL:
                low, high = halves(c, a, tile)
                at = (TILES_DEV + s) * TILE
                sets[a][q, at : at + TILE, :] = jnp.where(upper(y, q, s), high, low)
            for g, (group, _) in enumerate(GROUPS):
                for n, (q, s, _) in enumerate(group):
                    at = (TILES_DEV + s) * TILE
                    sets[a][q, at : at + TILE, :] = gots[g][c, a, n]

        head_row = tables[2 * x + lax.div(c, 3), pl.ds(lax.rem(c, 3), 1), :]
        for j in range(TILE_COLS):
            shifted[j : j + 1, :] = pltpu.roll(head_row, (2 * TABLE - BUCKETS - j) % TABLE, 1)
        for j in range(TILE_ROWS):
            shifted[TILE_COLS + j : TILE_COLS + j + 1, :] = pltpu.roll(
                head_row, (2 * TABLE - BUCKETS - COLUMN_WIDTH - j) % TABLE, 1
            )
        offset = iota((TABLE, TILE), 0)
        query_at = iota((TABLE, TILE), 1)
        column_hot = (offset == TILE_COLS - 1 - lax.rem(query_at, TILE_COLS)).astype(jnp.float32)
        row_hot = (offset == TILE_ROWS - 1 - lax.div(query_at, TILE_COLS)).astype(jnp.float32)
        column_bias = jnp.dot(
            shifted[0:TILE_COLS, :], column_hot, precision=HIGHEST,
            preferred_element_type=jnp.float32,
        )
        row_bias = jnp.dot(
            shifted[TILE_COLS : TILE_COLS + TILE_ROWS, :], row_hot, precision=HIGHEST,
            preferred_element_type=jnp.float32,
        )
        for j in range(TILE_ROWS):
            band = column_bias + row_bias[j : j + 1, :]
            fine[j * TILE_COLS : (j + 1) * TILE_COLS, 0:TILE] = band
            fine[j * TILE_COLS : (j + 1) * TILE_COLS, TILE : 2 * TILE] = band
        fine_sum[...] = jnp.zeros_like(fine_sum)
        coarse_sum[...] = jnp.zeros_like(coarse_sum)

        def one_query_tile(q, carry):
            query = qd_in[c, 0, q]
            grad = qd_in[c, 1, q]
            key = key_set[q]
            value = value_set[q]
            hot = entries[q, 0]
            entry_bias = jnp.sum(hot * head_row, axis=1, keepdims=True) + entries[q, 1][:, 0:1]
            both = (((1,), (1,)), ((), ()))
            raw = lax.dot_general(key, query, both, preferred_element_type=jnp.float32)
            product = lax.dot_general(value, grad, both, preferred_element_type=jnp.float32)
            fine_bias = fine[...]
            scores = [
                raw[e * TILE : (e + 1) * TILE, :] * SCALE + (fine_bias + entry_bias[e : e + 1, :])
                for e in range(ENTRIES)
            ]
            attend_grad = [product[e * TILE : (e + 1) * TILE, :] for e in range(ENTRIES)]
            top = scores[0]
            for e in range(1, ENTRIES):
                top = jnp.maximum(top, scores[e])
            top = jnp.max(top, axis=0, keepdims=True)
            expo = [jnp.exp(block - top) for block in scores]
            total, weighted = expo[0], expo[0] * attend_grad[0]
            for e in range(1, ENTRIES):
                total = total + expo[e]
                weighted = weighted + expo[e] * attend_grad[e]
            inverse = 1.0 / jnp.sum(total, axis=0, keepdims=True)
            delta = jnp.sum(weighted, axis=0, keepdims=True) * inverse
            attend = [block * inverse for block in expo]
            score_grad = [attend[e] * (attend_grad[e] - delta) for e in range(ENTRIES)]
            attend_low = jnp.concatenate([b.astype(jnp.bfloat16) for b in attend], axis=0)
            grad_low = jnp.concatenate([b.astype(jnp.bfloat16) for b in score_grad], axis=0)
            value_part[q] = jnp.dot(attend_low, grad, preferred_element_type=jnp.float32)
            key_part[q] = jnp.dot(grad_low, query, preferred_element_type=jnp.float32) * SCALE
            query_grad = lax.dot_general(
                key, grad_low, (((0,), (0,)), ((), ())), preferred_element_type=jnp.float32
            )
            ret[c, 0, q] = (query_grad.T * SCALE).astype(jnp.bfloat16)
            total_grad = score_grad[0]
            for e in range(1, ENTRIES):
                total_grad = total_grad + score_grad[e]
            fine_sum[...] += total_grad[:, 0:TILE] + total_grad[:, TILE : 2 * TILE]
            coarse = jnp.zeros((1, TABLE), jnp.float32)
            for e in range(ENTRIES):
                block_sum = jnp.sum(score_grad[e], axis=0, keepdims=True)
                coarse = coarse + jnp.sum(block_sum, axis=1, keepdims=True) * hot[e : e + 1, :]
            coarse_sum[0:1, :] += coarse
            return carry

        lax.fori_loop(0, SIDE, one_query_tile, 0)
        give_back(0, c)
        parts = (key_part, value_part)
        for g, (group, _) in enumerate(GROUPS):
            for n, (q, s, _) in enumerate(group):
                at = (TILES_DEV + s) * TILE
                for a in range(2):
                    backs[g][c, a, n] = parts[a][q, at : at + TILE, :].astype(jnp.bfloat16)
            back_copy(g, c).start()
        slot = lax.rem(c, 2)
        for a in range(2):
            for q in range(SIDE):
                acc[slot, a, q] = parts[a][q, 0 : 2 * TILE, :]
            for q, s, tile in LOCAL:
                at = (TILES_DEV + s) * TILE
                deposit(slot, a, tile, upper(y, q, s), parts[a][q, at : at + TILE, :])

        folded = fine_sum[...].reshape(TILE_ROWS, TILE_COLS, TILE)
        across = (((1,), (1,)), ((), ()))
        column_grad = lax.dot_general(
            jnp.sum(folded, axis=0), column_hot, across, precision=HIGHEST,
            preferred_element_type=jnp.float32,
        )
        row_grad = lax.dot_general(
            jnp.sum(folded, axis=1), row_hot, across, precision=HIGHEST,
            preferred_element_type=jnp.float32,
        )
        table_row = coarse_sum[0:1, :]
        for j in range(TILE_COLS):
            table_row = table_row + pltpu.roll(column_grad[j : j + 1, :], BUCKETS + j, 1)
        for j in range(TILE_ROWS):
            table_row = table_row + pltpu.roll(
                row_grad[j : j + 1, :], BUCKETS + COLUMN_WIDTH + j, 1
            )
        grads[pl.ds(c, 1), :] = table_row

    def deposit(slot, a, tile, pick, partial):
        acc[slot, a, tile, 0:TILE, :] += jnp.where(pick, 0.0, partial)
        acc[slot, a, tile, TILE : 2 * TILE, :] += jnp.where(pick, partial, 0.0)

    def finish(c):
        slot = lax.rem(c, 2)
        for g, (group, distance) in enumerate(GROUPS):
            arrived(homes[g].at[c], home_recv.at[c, g])
            for n, (q, s, tile) in enumerate(group):
                pick = upper(y + distance, q, s)
                for a in range(2):
                    deposit(slot, a, tile, pick, homes[g][c, a, n].astype(jnp.float32))
        for a in range(2):
            for q in range(SIDE):
                ret[c, 1 + a, q] = acc[slot, a, q].astype(jnp.bfloat16)
            give_back(1 + a, c)

    def dp_copy(j):
        return remote(
            grads, grads_dp.at[part], dp_send.at[j], dp_recv.at[part],
            {"dp": lax.rem(part + j, DP)},
        )

    def seq_copy(j):
        return remote(
            grads_seq.at[place], grads_seq.at[place], seq_send.at[j], seq_recv.at[place],
            {"seq": lax.rem(place + j, SEQ)},
        )

    def step(t, carry):
        @pl.when(t < CHUNKS)
        def _():
            send_tiles(t)

        @pl.when((t >= 1) & (t < CHUNKS + 1))
        def _():
            compute(t - 1)

        @pl.when(t >= 2)
        def _():
            finish(t - 2)

        return carry

    lax.fori_loop(0, CHUNKS + 1, step, 0)

    for j in range(1, DP):
        dp_copy(j).start()
    total = grads[...]
    for j in range(1, DP):
        source = lax.rem(part + j, DP)
        arrived(grads_dp.at[source], dp_recv.at[source])
        total = total + grads_dp[source]
    grads_seq[place] = total
    for j in range(1, SEQ):
        seq_copy(j).start()
    finish(CHUNKS - 1)
    for j in range(1, SEQ):
        source = lax.rem(place + j, SEQ)
        arrived(grads_seq.at[source], seq_recv.at[source])
    owner = lax.div(part, 2)
    mine = grads_seq[owner]
    for j in range(1, SIDE):
        mine = mine + grads_seq[owner + j * SIDE]
    own = HEADS // DP
    table_out[...] = jnp.where(lax.rem(part, 2) == 0, mine[0:own, :], mine[own : 2 * own, :])

    def drain(c, carry):
        for copy in in_copies(*kv, c) + in_copies(*qd, c):
            copy.wait_send()
        for g in range(3):
            give_copy(g, c).wait_send()
            back_copy(g, c).wait_send()
        for a in range(3):
            for copy in ret_copies(a, c):
                copy.wait_send()
        return carry

    lax.fori_loop(0, CHUNKS, drain, 0)
    for j in range(1, DP):
        table_copy(j).wait_send()
        dp_copy(j).wait_send()
    for j in range(1, SIDE):
        entry_copy(j).wait_send()
    for j in range(1, SEQ):
        seq_copy(j).wait_send()
    for a in range(3):
        arrived(outs[a], out_recv.at[a])


def per_device(queries, keys, values, grad_out, bias_table, slot_tiles, live, buckets):
    hbm = pl.BlockSpec(memory_space=pltpu.HBM)
    vmem = pl.BlockSpec(memory_space=pltpu.VMEM)
    smem = pl.BlockSpec(memory_space=pltpu.SMEM)
    low, full = jnp.bfloat16, jnp.float32
    dma = pltpu.SemaphoreType.DMA
    moved = [pltpu.VMEM((CHUNKS, 2, len(group), TILE, HEAD_DIM), low) for group, _ in GROUPS]
    set_rows = ENTRIES * TILE
    out = jax.ShapeDtypeStruct((TOK_DEV, WIDTH), low)
    result = pl.pallas_call(
        kernel,
        out_shape=(out, out, out, jax.ShapeDtypeStruct((HEADS // DP, TABLE), full)),
        in_specs=[hbm] * 4 + [vmem, smem, smem, smem],
        out_specs=(hbm, hbm, hbm, vmem),
        scratch_shapes=[
            pltpu.VMEM((CHUNKS, 2, SIDE, TOK_DEV, HEAD_DIM), low),
            pltpu.VMEM((CHUNKS, 2, SIDE, TOK_DEV, HEAD_DIM), low),
            *moved, *moved, *moved, *moved,
            pltpu.VMEM((CHUNKS, 3, SIDE, TOK_DEV, HEAD_DIM), low),
            pltpu.VMEM((2, 2, SIDE, TOK_DEV, HEAD_DIM), full),
            pltpu.VMEM((SIDE, set_rows, HEAD_DIM), low),
            pltpu.VMEM((SIDE, set_rows, HEAD_DIM), low),
            pltpu.VMEM((SIDE, set_rows, HEAD_DIM), full),
            pltpu.VMEM((SIDE, set_rows, HEAD_DIM), full),
            pltpu.VMEM((DP, 8, TABLE), full),
            pltpu.VMEM((SIDE, 2, 8, TABLE), full),
            pltpu.VMEM((TILE_COLS + TILE_ROWS, TABLE), full),
            pltpu.VMEM((TILE, 2 * TILE), full),
            pltpu.VMEM((TILE, TILE), full),
            pltpu.VMEM((8, TABLE), full),
            pltpu.VMEM((8, TABLE), full),
            pltpu.VMEM((DP, 8, TABLE), full),
            pltpu.VMEM((SEQ, 8, TABLE), full),
            dma((CHUNKS, 2, SIDE)), dma((CHUNKS,)),
            dma((CHUNKS, 2, SIDE)), dma((CHUNKS,)),
            dma((CHUNKS, 3)), dma((CHUNKS, 3)),
            dma((CHUNKS, 3)), dma((CHUNKS, 3)),
            dma((CHUNKS, 3, SIDE)), dma((3,)),
            dma((DP,)), dma((DP,)),
            dma((SIDE,)), dma((SIDE,)),
            dma((DP,)), dma((DP,)),
            dma((SEQ,)), dma((SEQ,)),
        ],
        compiler_params=pltpu.CompilerParams(
            collective_id=0, has_side_effects=True, vmem_limit_bytes=60 * 2**20
        ),
        cost_estimate=pl.CostEstimate(
            flops=7_046_430_720, bytes_accessed=11_000_000, transcendentals=5_505_024
        ),
    )(queries[0], keys[0], values[0], grad_out[0], bias_table, slot_tiles, live, buckets)
    query_grad, key_grad, value_grad, table_grad = result
    return (query_grad[None], key_grad[None], value_grad[None], table_grad)


def solution(mesh):
    rows = P("dp", "seq", None)
    return jax.shard_map(
        per_device,
        mesh=mesh,
        in_specs=(rows, rows, rows, rows, P("dp", None), P(), P("seq", None), P("seq", None)),
        out_specs=(rows, rows, rows, P("dp", None)),
        check_vma=False,
    )
```

```python
import jax
import jax.numpy as jnp
from jax import lax
from jax.experimental import pallas as pl
from jax.experimental.pallas import tpu as pltpu
from jax.sharding import PartitionSpec as P

HEADS = 24
HEAD_DIM = 128
TOK_DEV = 256
TILE = 128
TILE_COLS = 16
TILE_ROWS = TILE // TILE_COLS
SLOTS = 5
BUCKETS = 82
WIDTH = 3072
TILES_DEV = 2
ENTRIES = TILES_DEV + SLOTS
COLUMN_WIDTH = 2 * TILE_COLS - 1
TABLE = 128

SIDE = 4
SEQ = SIDE * SIDE
DP = 8
CHUNKS = HEADS // SIDE
NEGATIVE = -1e30
SCALE = HEAD_DIM ** (-0.5)
NEAR_OFFSETS = (-1, 1, -2, 2)
HIGHEST = lax.Precision.HIGHEST
MESH = pl.DeviceIdType.MESH

FROM_BELOW = tuple((q, s, q + o + SIDE) for q in range(SIDE) for s, o in enumerate(NEAR_OFFSETS) if q + o < 0)
FROM_ABOVE = tuple((q, s, q + o - SIDE) for q in range(SIDE) for s, o in enumerate(NEAR_OFFSETS) if q + o >= SIDE)
FROM_HALF = tuple((q, SLOTS - 1, q) for q in range(SIDE))
GROUPS = ((FROM_BELOW, 1), (FROM_ABOVE, SIDE - 1), (FROM_HALF, SIDE // 2))
LOCAL = tuple(
    (q, s, q + o) for q in range(SIDE) for s, o in enumerate(NEAR_OFFSETS) if 0 <= q + o < SIDE
)


def iota(shape, axis):
    return lax.broadcasted_iota(jnp.int32, shape, axis)


def kernel(
    queries, keys, values, upstream, table, slots_hbm, live_hbm, buckets_hbm,
    query_out, key_out, value_out, table_out,
    kv_in, qd_in, give0, give1, give2, got0, got1, got2, back0, back1, back2, home0, home1, home2,
    ret, acc, key_set, value_set, key_part, value_part,
    slots, live, buckets, own_heads, direct,
    tables, entries, shifted, fine, fine_sum, coarse_sum, grads, grads_dp, grads_seq,
    small_recv, own_recv,
    kv_send, kv_recv, qd_send, qd_recv, give_send, got_recv, back_send, home_recv, ret_send, out_recv,
    table_send, table_recv, entry_send, entry_recv, dp_send, dp_recv, seq_send, seq_recv,
):
    gives, gots = (give0, give1, give2), (got0, got1, got2)
    backs, homes = (back0, back1, back2), (home0, home1, home2)
    outs = (query_out, key_out, value_out)
    place = lax.axis_index("seq")
    part = lax.axis_index("dp")
    x, y = lax.rem(place, SIDE), lax.div(place, SIDE)

    def seq_at(column, row):
        return {"seq": lax.rem(row, SIDE) * SIDE + lax.rem(column, SIDE)}

    def remote(source, target, send, recv, device):
        return pltpu.make_async_remote_copy(
            src_ref=source, dst_ref=target, send_sem=send, recv_sem=recv,
            device_id=device, device_id_type=MESH,
        )

    def arrived(buffer, semaphore):
        pltpu.make_async_copy(buffer, buffer, semaphore).wait()

    def head_columns(head):
        return pl.ds(pl.multiple_of(head * HEAD_DIM, HEAD_DIM), HEAD_DIM)

    barrier = pltpu.get_barrier_semaphore()
    for j in range(1, SEQ):
        pl.semaphore_signal(
            barrier, inc=1, device_id={"seq": lax.rem(place + j, SEQ)}, device_id_type=MESH
        )
    for j in range(1, DP):
        pl.semaphore_signal(
            barrier, inc=1, device_id={"dp": lax.rem(part + j, DP)}, device_id_type=MESH
        )

    small = [
        pltpu.make_async_copy(source, target, small_recv.at[n])
        for n, (source, target) in enumerate(
            ((slots_hbm, slots), (live_hbm, live), (buckets_hbm, buckets))
        )
    ]
    for copy in small:
        copy.start()
    for a, ref in enumerate((keys, values)):
        for to in range(SIDE):
            pltpu.make_async_copy(
                ref.at[:, head_columns(to * CHUNKS)], own_heads.at[a, to], own_recv
            ).start()
    for copy in small:
        copy.wait()

    def upper(query_row, q, s):
        return lax.rem(slots[s, lax.rem(query_row, SIDE) * SIDE + q], TILES_DEV) == 1

    lane = iota((8, TABLE), 1)
    row = iota((8, TABLE), 0)
    tables[part] = jnp.zeros((8, TABLE), jnp.float32)
    tables[part, 0 : HEADS // DP, :] = table[...]
    bucket = jnp.full((8, TABLE), -1, jnp.int32)
    alive = jnp.zeros((8, TABLE), jnp.int32)
    for e in range(ENTRIES):
        bucket = jnp.where(row == e, buckets[0, e], bucket)
        alive = jnp.where(row == e, live[0, e], alive)
    entries[x, 0] = (lane == bucket).astype(jnp.float32)
    entries[x, 1] = jnp.where(alive > 0, 0.0, NEGATIVE)
    grads[...] = jnp.zeros_like(grads)
    arrived(own_heads, own_recv)
    half_pick = upper(y + SIDE // 2, x, SLOTS - 1)
    for a in range(2):
        for to in range(SIDE):
            direct[a, to] = jnp.where(
                half_pick, own_heads[a, to, TILE : 2 * TILE, :], own_heads[a, to, 0:TILE, :]
            )

    pl.semaphore_wait(barrier, SEQ - 1 + DP - 1)

    def table_copy(j):
        return remote(
            tables.at[part], tables.at[part], table_send.at[j], table_recv.at[part],
            {"dp": lax.rem(part + j, DP)},
        )

    def entry_copy(j):
        return remote(
            entries.at[x], entries.at[x], entry_send.at[j], entry_recv.at[x], seq_at(x + j, y)
        )

    def fetch(refs, buffer, send, recv, c):
        for a, ref in enumerate(refs):
            for j in (2, 1, 3):
                to = lax.rem(x + j, SIDE)
                remote(
                    ref.at[:, head_columns(to * CHUNKS + c)], buffer.at[c, a, x],
                    send, recv.at[c, a], seq_at(to, y),
                ).start()
            pltpu.make_async_copy(
                ref.at[:, head_columns(x * CHUNKS + c)], buffer.at[c, a, x], recv.at[c, a]
            ).start()

    kv = ((keys, values), kv_in, kv_send, kv_recv)
    qd = ((queries, upstream), qd_in, qd_send, qd_recv)

    def give_copy(g, c, a):
        return remote(
            gives[g].at[c, a], gots[g].at[c, a], give_send.at[g], got_recv.at[c, g, a],
            seq_at(x, y + GROUPS[g][1]),
        )

    def back_copy(g, c, a):
        return remote(
            backs[g].at[c, a], homes[g].at[c, a], back_send.at[g], home_recv.at[c, g, a],
            seq_at(x, y + SIDE - GROUPS[g][1]),
        )

    def give_back(a, c):
        columns = head_columns(x * CHUNKS + c)
        for j in (2, 1, 3):
            remote(
                ret.at[c, a, lax.rem(x + j, SIDE)], outs[a].at[:, columns],
                ret_send.at[a], out_recv.at[a], seq_at(x + j, y),
            ).start()
        pltpu.make_async_copy(ret.at[c, a, x], outs[a].at[:, columns], out_recv.at[a]).start()

    for a in range(2):
        for to in range(SIDE):
            remote(
                direct.at[a, to], gots[2].at[0, a, x], give_send.at[2], got_recv.at[0, 2, a],
                seq_at(to, y + SIDE // 2),
            ).start()
    fetch(*kv, 0)
    for j in range(1, DP):
        table_copy(j).start()
    for j in range(1, SIDE):
        entry_copy(j).start()
    fetch(*kv, 1)
    fetch(*qd, 0)

    def halves(c, a, tile):
        return kv_in[c, a, tile, 0:TILE, :], kv_in[c, a, tile, TILE : 2 * TILE, :]

    def send_tiles(c):
        for a in range(2):
            arrived(kv_in.at[c, a], kv_recv.at[c, a])
            for g, (group, distance) in enumerate(GROUPS):

                def give(g=g, group=group, distance=distance):
                    for n, (q, s, tile) in enumerate(group):
                        low, high = halves(c, a, tile)
                        gives[g][c, a, n] = jnp.where(upper(y + distance, q, s), high, low)
                    give_copy(g, c, a).start()

                if g < 2:
                    give()
                else:
                    pl.when(c > 0)(give)

        @pl.when(c + 2 < CHUNKS)
        def _():
            fetch(*kv, c + 2)

        @pl.when(c + 1 < CHUNKS)
        def _():
            fetch(*qd, c + 1)

    def compute(c):
        for a in range(2):
            arrived(qd_in.at[c, a], qd_recv.at[c, a])
            for g in range(3):
                arrived(gots[g].at[c, a], got_recv.at[c, g, a])
        sets = (key_set, value_set)
        for a in range(2):
            for q in range(SIDE):
                sets[a][q, 0 : 2 * TILE, :] = kv_in[c, a, q]
            for q, s, tile in LOCAL:
                low, high = halves(c, a, tile)
                at = (TILES_DEV + s) * TILE
                sets[a][q, at : at + TILE, :] = jnp.where(upper(y, q, s), high, low)
            for g, (group, _) in enumerate(GROUPS):
                for n, (q, s, _) in enumerate(group):
                    at = (TILES_DEV + s) * TILE
                    sets[a][q, at : at + TILE, :] = gots[g][c, a, n]

        head_row = tables[2 * x + lax.div(c, 3), pl.ds(lax.rem(c, 3), 1), :]
        for j in range(TILE_COLS):
            shifted[j : j + 1, :] = pltpu.roll(head_row, (2 * TABLE - BUCKETS - j) % TABLE, 1)
        for j in range(TILE_ROWS):
            shifted[TILE_COLS + j : TILE_COLS + j + 1, :] = pltpu.roll(
                head_row, (2 * TABLE - BUCKETS - COLUMN_WIDTH - j) % TABLE, 1
            )
        offset = iota((TABLE, TILE), 0)
        query_at = iota((TABLE, TILE), 1)
        column_hot = (offset == TILE_COLS - 1 - lax.rem(query_at, TILE_COLS)).astype(jnp.float32)
        row_hot = (offset == TILE_ROWS - 1 - lax.div(query_at, TILE_COLS)).astype(jnp.float32)
        column_bias = jnp.dot(
            shifted[0:TILE_COLS, :], column_hot, precision=HIGHEST,
            preferred_element_type=jnp.float32,
        )
        row_bias = jnp.dot(
            shifted[TILE_COLS : TILE_COLS + TILE_ROWS, :], row_hot, precision=HIGHEST,
            preferred_element_type=jnp.float32,
        )
        for j in range(TILE_ROWS):
            band = column_bias + row_bias[j : j + 1, :]
            fine[j * TILE_COLS : (j + 1) * TILE_COLS, 0:TILE] = band
            fine[j * TILE_COLS : (j + 1) * TILE_COLS, TILE : 2 * TILE] = band
        fine_sum[...] = jnp.zeros_like(fine_sum)
        coarse_sum[...] = jnp.zeros_like(coarse_sum)

        def one_query_tile(q, carry):
            query = qd_in[c, 0, q]
            grad = qd_in[c, 1, q]
            key = key_set[q]
            value = value_set[q]
            hot = entries[q, 0]
            entry_bias = jnp.sum(hot * head_row, axis=1, keepdims=True) + entries[q, 1][:, 0:1]
            both = (((1,), (1,)), ((), ()))
            raw = lax.dot_general(key, query, both, preferred_element_type=jnp.float32)
            product = lax.dot_general(value, grad, both, preferred_element_type=jnp.float32)
            fine_bias = fine[...]
            scores = [
                raw[e * TILE : (e + 1) * TILE, :] * SCALE + (fine_bias + entry_bias[e : e + 1, :])
                for e in range(ENTRIES)
            ]
            attend_grad = [product[e * TILE : (e + 1) * TILE, :] for e in range(ENTRIES)]
            top = scores[0]
            for e in range(1, ENTRIES):
                top = jnp.maximum(top, scores[e])
            top = jnp.max(top, axis=0, keepdims=True)
            expo = [jnp.exp(block - top) for block in scores]
            total, weighted = expo[0], expo[0] * attend_grad[0]
            for e in range(1, ENTRIES):
                total = total + expo[e]
                weighted = weighted + expo[e] * attend_grad[e]
            inverse = 1.0 / jnp.sum(total, axis=0, keepdims=True)
            delta = jnp.sum(weighted, axis=0, keepdims=True) * inverse
            attend = [block * inverse for block in expo]
            score_grad = [attend[e] * (attend_grad[e] - delta) for e in range(ENTRIES)]
            attend_low = jnp.concatenate([b.astype(jnp.bfloat16) for b in attend], axis=0)
            grad_low = jnp.concatenate([b.astype(jnp.bfloat16) for b in score_grad], axis=0)
            value_part[q] = jnp.dot(attend_low, grad, preferred_element_type=jnp.float32)
            key_part[q] = jnp.dot(grad_low, query, preferred_element_type=jnp.float32) * SCALE
            query_grad = lax.dot_general(
                key, grad_low, (((0,), (0,)), ((), ())), preferred_element_type=jnp.float32
            )
            ret[c, 0, q] = (query_grad.T * SCALE).astype(jnp.bfloat16)
            total_grad = score_grad[0]
            for e in range(1, ENTRIES):
                total_grad = total_grad + score_grad[e]
            fine_sum[...] += total_grad[:, 0:TILE] + total_grad[:, TILE : 2 * TILE]
            coarse = jnp.zeros((1, TABLE), jnp.float32)
            for e in range(ENTRIES):
                block_sum = jnp.sum(score_grad[e], axis=0, keepdims=True)
                coarse = coarse + jnp.sum(block_sum, axis=1, keepdims=True) * hot[e : e + 1, :]
            coarse_sum[0:1, :] += coarse
            return carry

        lax.fori_loop(0, SIDE, one_query_tile, 0)
        give_back(0, c)
        parts = (key_part, value_part)
        for a in range(2):
            for g, (group, _) in enumerate(GROUPS):
                for n, (q, s, _) in enumerate(group):
                    at = (TILES_DEV + s) * TILE
                    backs[g][c, a, n] = parts[a][q, at : at + TILE, :].astype(jnp.bfloat16)
                back_copy(g, c, a).start()
        slot = lax.rem(c, 2)
        for a in range(2):
            for q in range(SIDE):
                acc[slot, a, q] = parts[a][q, 0 : 2 * TILE, :]
            for q, s, tile in LOCAL:
                at = (TILES_DEV + s) * TILE
                deposit(slot, a, tile, upper(y, q, s), parts[a][q, at : at + TILE, :])

        folded = fine_sum[...].reshape(TILE_ROWS, TILE_COLS, TILE)
        across = (((1,), (1,)), ((), ()))
        column_grad = lax.dot_general(
            jnp.sum(folded, axis=0), column_hot, across, precision=HIGHEST,
            preferred_element_type=jnp.float32,
        )
        row_grad = lax.dot_general(
            jnp.sum(folded, axis=1), row_hot, across, precision=HIGHEST,
            preferred_element_type=jnp.float32,
        )
        table_row = coarse_sum[0:1, :]
        for j in range(TILE_COLS):
            table_row = table_row + pltpu.roll(column_grad[j : j + 1, :], BUCKETS + j, 1)
        for j in range(TILE_ROWS):
            table_row = table_row + pltpu.roll(
                row_grad[j : j + 1, :], BUCKETS + COLUMN_WIDTH + j, 1
            )
        grads[pl.ds(c, 1), :] = table_row

    def deposit(slot, a, tile, pick, partial):
        acc[slot, a, tile, 0:TILE, :] += jnp.where(pick, 0.0, partial)
        acc[slot, a, tile, TILE : 2 * TILE, :] += jnp.where(pick, partial, 0.0)

    def finish(c):
        slot = lax.rem(c, 2)
        for a in range(2):
            for g, (group, distance) in enumerate(GROUPS):
                arrived(homes[g].at[c, a], home_recv.at[c, g, a])
                for n, (q, s, tile) in enumerate(group):
                    deposit(
                        slot, a, tile, upper(y + distance, q, s),
                        homes[g][c, a, n].astype(jnp.float32),
                    )
            for q in range(SIDE):
                ret[c, 1 + a, q] = acc[slot, a, q].astype(jnp.bfloat16)
            give_back(1 + a, c)

    def dp_copy(j):
        return remote(
            grads, grads_dp.at[part], dp_send.at[j], dp_recv.at[part],
            {"dp": lax.rem(part + j, DP)},
        )

    def seq_copy(j):
        return remote(
            grads_seq.at[place], grads_seq.at[place], seq_send.at[j], seq_recv.at[place],
            {"seq": lax.rem(place + j, SEQ)},
        )

    def step(t, carry):
        @pl.when(t < CHUNKS)
        def _():
            send_tiles(t)

        @pl.when(t == 1)
        def _():
            for j in range(1, DP):
                source = lax.rem(part + j, DP)
                arrived(tables.at[source], table_recv.at[source])
            for j in range(1, SIDE):
                source = lax.rem(x + j, SIDE)
                arrived(entries.at[source], entry_recv.at[source])

        @pl.when(t >= 1)
        def _():
            compute(t - 1)

        @pl.when(t >= 2)
        def _():
            finish(t - 2)

        return carry

    lax.fori_loop(0, CHUNKS + 1, step, 0)

    for j in range(1, DP):
        dp_copy(j).start()
    total = grads[...]
    for j in range(1, DP):
        source = lax.rem(part + j, DP)
        arrived(grads_dp.at[source], dp_recv.at[source])
        total = total + grads_dp[source]
    grads_seq[place] = total
    for j in range(1, SEQ):
        seq_copy(j).start()
    finish(CHUNKS - 1)
    for j in range(1, SEQ):
        source = lax.rem(place + j, SEQ)
        arrived(grads_seq.at[source], seq_recv.at[source])
    owner = lax.div(part, 2)
    mine = grads_seq[owner]
    for j in range(1, SIDE):
        mine = mine + grads_seq[owner + j * SIDE]
    own = HEADS // DP
    table_out[...] = jnp.where(lax.rem(part, 2) == 0, mine[0:own, :], mine[own : 2 * own, :])

    peers = slice(0, SIDE - 1)
    arrived(kv_in.at[:, :, peers], kv_send)
    arrived(qd_in.at[:, :, peers], qd_send)
    for g in range(3):
        arrived(gives[g], give_send.at[g])
        arrived(backs[g], back_send.at[g])
    for a in range(3):
        arrived(ret.at[:, a, peers], ret_send.at[a])
    for j in range(1, DP):
        table_copy(j).wait_send()
        dp_copy(j).wait_send()
    for j in range(1, SIDE):
        entry_copy(j).wait_send()
    for j in range(1, SEQ):
        seq_copy(j).wait_send()
    for a in range(3):
        arrived(outs[a], out_recv.at[a])


def per_device(queries, keys, values, grad_out, bias_table, slot_tiles, live, buckets):
    hbm = pl.BlockSpec(memory_space=pltpu.HBM)
    vmem = pl.BlockSpec(memory_space=pltpu.VMEM)
    low, full = jnp.bfloat16, jnp.float32
    dma = pltpu.SemaphoreType.DMA
    moved = [pltpu.VMEM((CHUNKS, 2, len(group), TILE, HEAD_DIM), low) for group, _ in GROUPS]
    set_rows = ENTRIES * TILE
    out = jax.ShapeDtypeStruct((TOK_DEV, WIDTH), low)
    result = pl.pallas_call(
        kernel,
        out_shape=(out, out, out, jax.ShapeDtypeStruct((HEADS // DP, TABLE), full)),
        in_specs=[hbm] * 4 + [vmem, hbm, hbm, hbm],
        out_specs=(hbm, hbm, hbm, vmem),
        scratch_shapes=[
            pltpu.VMEM((CHUNKS, 2, SIDE, TOK_DEV, HEAD_DIM), low),
            pltpu.VMEM((CHUNKS, 2, SIDE, TOK_DEV, HEAD_DIM), low),
            *moved, *moved, *moved, *moved,
            pltpu.VMEM((CHUNKS, 3, SIDE, TOK_DEV, HEAD_DIM), low),
            pltpu.VMEM((2, 2, SIDE, TOK_DEV, HEAD_DIM), full),
            pltpu.VMEM((SIDE, set_rows, HEAD_DIM), low),
            pltpu.VMEM((SIDE, set_rows, HEAD_DIM), low),
            pltpu.VMEM((SIDE, set_rows, HEAD_DIM), full),
            pltpu.VMEM((SIDE, set_rows, HEAD_DIM), full),
            pltpu.SMEM((SLOTS, SEQ), jnp.int32),
            pltpu.SMEM(live.shape, jnp.int32),
            pltpu.SMEM(buckets.shape, jnp.int32),
            pltpu.VMEM((2, SIDE, TOK_DEV, HEAD_DIM), low),
            pltpu.VMEM((2, SIDE, TILE, HEAD_DIM), low),
            pltpu.VMEM((DP, 8, TABLE), full),
            pltpu.VMEM((SIDE, 2, 8, TABLE), full),
            pltpu.VMEM((TILE_COLS + TILE_ROWS, TABLE), full),
            pltpu.VMEM((TILE, 2 * TILE), full),
            pltpu.VMEM((TILE, TILE), full),
            pltpu.VMEM((8, TABLE), full),
            pltpu.VMEM((8, TABLE), full),
            pltpu.VMEM((DP, 8, TABLE), full),
            pltpu.VMEM((SEQ, 8, TABLE), full),
            dma((3,)), dma(()),
            dma(()), dma((CHUNKS, 2)),
            dma(()), dma((CHUNKS, 2)),
            dma((3,)), dma((CHUNKS, 3, 2)),
            dma((3,)), dma((CHUNKS, 3, 2)),
            dma((3,)), dma((3,)),
            dma((DP,)), dma((DP,)),
            dma((SIDE,)), dma((SIDE,)),
            dma((DP,)), dma((DP,)),
            dma((SEQ,)), dma((SEQ,)),
        ],
        compiler_params=pltpu.CompilerParams(
            collective_id=0, has_side_effects=True, vmem_limit_bytes=60 * 2**20
        ),
        cost_estimate=pl.CostEstimate(
            flops=7_046_430_720, bytes_accessed=11_000_000, transcendentals=5_505_024
        ),
    )(queries[0], keys[0], values[0], grad_out[0], bias_table, slot_tiles.T, live, buckets)
    query_grad, key_grad, value_grad, table_grad = result
    return (query_grad[None], key_grad[None], value_grad[None], table_grad)


def solution(mesh):
    rows = P("dp", "seq", None)
    return jax.shard_map(
        per_device,
        mesh=mesh,
        in_specs=(rows, rows, rows, rows, P("dp", None), P(), P("seq", None), P("seq", None)),
        out_specs=(rows, rows, rows, P("dp", None)),
        check_vma=False,
    )
```

```python
import jax
import jax.numpy as jnp
from jax import lax
from jax.experimental import pallas as pl
from jax.experimental.pallas import tpu as pltpu
from jax.sharding import PartitionSpec as P

HEADS = 24
HEAD_DIM = 128
TOK_DEV = 256
TILE = 128
TILE_COLS = 16
TILE_ROWS = TILE // TILE_COLS
SLOTS = 5
BUCKETS = 82
WIDTH = 3072
TILES_DEV = 2
ENTRIES = TILES_DEV + SLOTS
COLUMN_WIDTH = 2 * TILE_COLS - 1
TABLE = 128

SIDE = 4
SEQ = SIDE * SIDE
DP = 8
CHUNKS = HEADS // SIDE
NEGATIVE = -1e30
SCALE = HEAD_DIM ** (-0.5)
NEAR_OFFSETS = (-1, 1, -2, 2)
HIGHEST = lax.Precision.HIGHEST
MESH = pl.DeviceIdType.MESH

ORDER = (2, 1, 3, 0)

FROM_BELOW = tuple((q, s, q + o + SIDE) for q in range(SIDE) for s, o in enumerate(NEAR_OFFSETS) if q + o < 0)
FROM_ABOVE = tuple((q, s, q + o - SIDE) for q in range(SIDE) for s, o in enumerate(NEAR_OFFSETS) if q + o >= SIDE)
FROM_HALF = tuple((q, SLOTS - 1, q) for q in range(SIDE))
GROUPS = ((FROM_BELOW, 1), (FROM_ABOVE, SIDE - 1), (FROM_HALF, SIDE // 2))
LOCAL = tuple(
    (q, s, q + o) for q in range(SIDE) for s, o in enumerate(NEAR_OFFSETS) if 0 <= q + o < SIDE
)


def iota(shape, axis):
    return lax.broadcasted_iota(jnp.int32, shape, axis)


def kernel(
    queries, keys, values, upstream, table, slots_hbm, live_hbm, buckets_hbm,
    query_out, key_out, value_out, table_out,
    kv_in, qd_in, give0, give1, give2, got0, got1, got2, back0, back1, back2, home0, home1, home2,
    ret, acc, key_set, value_set, key_part, value_part,
    slots, live, buckets, own_heads, direct, own_later, later,
    tables, entries, shifted, fine, fine_sum, coarse_sum, grads, grads_dp, grads_seq,
    small_recv, own_recv, later_recv,
    kv_send, kv_recv, qd_send, qd_recv, give_send, got_recv, back_send, home_recv, far_recv, ret_send, out_recv,
    table_send, table_recv, entry_send, entry_recv, dp_send, dp_recv, seq_send, seq_recv,
):
    gives, gots = (give0, give1, give2), (got0, got1, got2)
    backs, homes = (back0, back1, back2), (home0, home1, home2)
    outs = (query_out, key_out, value_out)
    place = lax.axis_index("seq")
    part = lax.axis_index("dp")
    x, y = lax.rem(place, SIDE), lax.div(place, SIDE)

    def seq_at(column, row):
        return {"seq": lax.rem(row, SIDE) * SIDE + lax.rem(column, SIDE)}

    def remote(source, target, send, recv, device):
        return pltpu.make_async_remote_copy(
            src_ref=source, dst_ref=target, send_sem=send, recv_sem=recv,
            device_id=device, device_id_type=MESH,
        )

    def arrived(buffer, semaphore):
        pltpu.make_async_copy(buffer, buffer, semaphore).wait()

    def head_columns(head):
        return pl.ds(pl.multiple_of(head * HEAD_DIM, HEAD_DIM), HEAD_DIM)

    barrier = pltpu.get_barrier_semaphore()
    for j in range(1, SEQ):
        pl.semaphore_signal(
            barrier, inc=1, device_id={"seq": lax.rem(place + j, SEQ)}, device_id_type=MESH
        )
    for j in range(1, DP):
        pl.semaphore_signal(
            barrier, inc=1, device_id={"dp": lax.rem(part + j, DP)}, device_id_type=MESH
        )

    small = [
        pltpu.make_async_copy(source, target, small_recv.at[n])
        for n, (source, target) in enumerate(
            ((slots_hbm, slots), (live_hbm, live), (buckets_hbm, buckets))
        )
    ]
    for copy in small:
        copy.start()
    for a, ref in enumerate((keys, values)):
        for to in range(SIDE):
            pltpu.make_async_copy(
                ref.at[:, head_columns(to * CHUNKS)], own_heads.at[a, to], own_recv
            ).start()
        for c in range(1, CHUNKS):
            pltpu.make_async_copy(
                ref.at[:, head_columns(x * CHUNKS + c)], own_later.at[a, c - 1], later_recv
            ).start()
    for copy in small:
        copy.wait()

    def upper(query_row, q, s):
        return lax.rem(slots[s, lax.rem(query_row, SIDE) * SIDE + q], TILES_DEV) == 1

    lane = iota((8, TABLE), 1)
    row = iota((8, TABLE), 0)
    tables[part] = jnp.zeros((8, TABLE), jnp.float32)
    tables[part, 0 : HEADS // DP, :] = table[...]
    bucket = jnp.full((8, TABLE), -1, jnp.int32)
    alive = jnp.zeros((8, TABLE), jnp.int32)
    for e in range(ENTRIES):
        bucket = jnp.where(row == e, buckets[0, e], bucket)
        alive = jnp.where(row == e, live[0, e], alive)
    entries[x, 0] = (lane == bucket).astype(jnp.float32)
    entries[x, 1] = jnp.where(alive > 0, 0.0, NEGATIVE)
    grads[...] = jnp.zeros_like(grads)
    arrived(own_heads, own_recv)
    half_pick = upper(y + SIDE // 2, x, SLOTS - 1)
    for a in range(2):
        for to in range(SIDE):
            direct[a, to] = jnp.where(
                half_pick, own_heads[a, to, TILE : 2 * TILE, :], own_heads[a, to, 0:TILE, :]
            )
    arrived(own_later, later_recv)
    for a in range(2):
        for c in range(CHUNKS - 1):
            later[a, c] = jnp.where(
                half_pick, own_later[a, c, TILE : 2 * TILE, :], own_later[a, c, 0:TILE, :]
            )

    pl.semaphore_wait(barrier, SEQ - 1 + DP - 1)

    def table_copy(j):
        return remote(
            tables.at[part], tables.at[part], table_send.at[j], table_recv.at[part],
            {"dp": lax.rem(part + j, DP)},
        )

    def entry_copy(j):
        return remote(
            entries.at[x], entries.at[x], entry_send.at[j], entry_recv.at[x], seq_at(x + j, y)
        )

    def fetch(refs, buffer, send, recv, c):
        for a, ref in enumerate(refs):
            for j in ORDER[:-1]:
                to = lax.rem(x + j, SIDE)
                remote(
                    ref.at[:, head_columns(to * CHUNKS + c)], buffer.at[c, a, x],
                    send, recv.at[c, a], seq_at(to, y),
                ).start()
            pltpu.make_async_copy(
                ref.at[:, head_columns(x * CHUNKS + c)], buffer.at[c, a, x], recv.at[c, a]
            ).start()

    kv = ((keys, values), kv_in, kv_send, kv_recv)
    qd = ((queries, upstream), qd_in, qd_send, qd_recv)

    def give_copy(g, c, a):
        return remote(
            gives[g].at[c, a], gots[g].at[c, a], give_send.at[g], got_recv.at[c, g, a],
            seq_at(x, y + GROUPS[g][1]),
        )

    def back_copy(g, c, a):
        return remote(
            backs[g].at[c, a], homes[g].at[c, a], back_send.at[g], home_recv.at[c, g, a],
            seq_at(x, y + SIDE - GROUPS[g][1]),
        )

    def far_back(c, a, tile):
        return remote(
            backs[2].at[c, a, tile], homes[2].at[c, a, tile], back_send.at[2],
            far_recv.at[c, a, tile], seq_at(x, y + SIDE // 2),
        )

    def give_back(a, c, j):
        columns = head_columns(x * CHUNKS + c)
        source = ret.at[c, a, lax.rem(x + j, SIDE)]
        if j == 0:
            pltpu.make_async_copy(source, outs[a].at[:, columns], out_recv.at[a]).start()
        else:
            remote(
                source, outs[a].at[:, columns], ret_send.at[a], out_recv.at[a], seq_at(x + j, y)
            ).start()

    for a in range(2):
        for to in range(SIDE):
            remote(
                direct.at[a, to], gots[2].at[0, a, x], give_send.at[2], got_recv.at[0, 2, a],
                seq_at(to, y + SIDE // 2),
            ).start()
    fetch(*kv, 0)
    for c in range(1, CHUNKS):
        for a in range(2):
            remote(
                later.at[a, c - 1], gots[2].at[c, a, x], give_send.at[2], got_recv.at[c, 2, a],
                seq_at(x, y + SIDE // 2),
            ).start()
    for j in range(1, DP):
        table_copy(j).start()
    for j in range(1, SIDE):
        entry_copy(j).start()
    fetch(*kv, 1)
    fetch(*kv, 2)
    fetch(*qd, 0)

    def halves(c, a, tile):
        return kv_in[c, a, tile, 0:TILE, :], kv_in[c, a, tile, TILE : 2 * TILE, :]

    def send_tiles(c):
        for a in range(2):
            arrived(kv_in.at[c, a], kv_recv.at[c, a])
            for g, (group, distance) in enumerate(GROUPS[:2]):
                for n, (q, s, tile) in enumerate(group):
                    low, high = halves(c, a, tile)
                    gives[g][c, a, n] = jnp.where(upper(y + distance, q, s), high, low)
                give_copy(g, c, a).start()

            @pl.when(c > 0)
            def _():
                for j in ORDER[:-1]:
                    tile = lax.rem(x + j, SIDE)
                    low, high = halves(c, a, tile)
                    pick = upper(y + SIDE // 2, tile, SLOTS - 1)
                    gives[2][c, a, tile] = jnp.where(pick, high, low)
                    remote(
                        gives[2].at[c, a, tile], gots[2].at[c, a, tile], give_send.at[2],
                        got_recv.at[c, 2, a], seq_at(x, y + SIDE // 2),
                    ).start()

        @pl.when(c + 3 < CHUNKS)
        def _():
            fetch(*kv, c + 3)

        @pl.when(c + 1 < CHUNKS)
        def _():
            fetch(*qd, c + 1)

    def compute(c):
        for a in range(2):
            arrived(qd_in.at[c, a], qd_recv.at[c, a])
            for g in range(3):
                arrived(gots[g].at[c, a], got_recv.at[c, g, a])
        sets = (key_set, value_set)
        for a in range(2):
            for q in range(SIDE):
                sets[a][q, 0 : 2 * TILE, :] = kv_in[c, a, q]
            for q, s, tile in LOCAL:
                low, high = halves(c, a, tile)
                at = (TILES_DEV + s) * TILE
                sets[a][q, at : at + TILE, :] = jnp.where(upper(y, q, s), high, low)
            for g, (group, _) in enumerate(GROUPS):
                for n, (q, s, _) in enumerate(group):
                    at = (TILES_DEV + s) * TILE
                    sets[a][q, at : at + TILE, :] = gots[g][c, a, n]

        head_row = tables[2 * x + lax.div(c, 3), pl.ds(lax.rem(c, 3), 1), :]
        for j in range(TILE_COLS):
            shifted[j : j + 1, :] = pltpu.roll(head_row, (2 * TABLE - BUCKETS - j) % TABLE, 1)
        for j in range(TILE_ROWS):
            shifted[TILE_COLS + j : TILE_COLS + j + 1, :] = pltpu.roll(
                head_row, (2 * TABLE - BUCKETS - COLUMN_WIDTH - j) % TABLE, 1
            )
        offset = iota((TABLE, TILE), 0)
        query_at = iota((TABLE, TILE), 1)
        column_hot = (offset == TILE_COLS - 1 - lax.rem(query_at, TILE_COLS)).astype(jnp.float32)
        row_hot = (offset == TILE_ROWS - 1 - lax.div(query_at, TILE_COLS)).astype(jnp.float32)
        column_bias = jnp.dot(
            shifted[0:TILE_COLS, :], column_hot, precision=HIGHEST,
            preferred_element_type=jnp.float32,
        )
        row_bias = jnp.dot(
            shifted[TILE_COLS : TILE_COLS + TILE_ROWS, :], row_hot, precision=HIGHEST,
            preferred_element_type=jnp.float32,
        )
        for j in range(TILE_ROWS):
            band = column_bias + row_bias[j : j + 1, :]
            fine[j * TILE_COLS : (j + 1) * TILE_COLS, 0:TILE] = band
            fine[j * TILE_COLS : (j + 1) * TILE_COLS, TILE : 2 * TILE] = band
        fine_sum[...] = jnp.zeros_like(fine_sum)
        coarse_sum[...] = jnp.zeros_like(coarse_sum)

        def one_query_tile(q, carry):
            query = qd_in[c, 0, q]
            grad = qd_in[c, 1, q]
            key = key_set[q]
            value = value_set[q]
            hot = entries[q, 0]
            entry_bias = jnp.sum(hot * head_row, axis=1, keepdims=True) + entries[q, 1][:, 0:1]
            both = (((1,), (1,)), ((), ()))
            raw = lax.dot_general(key, query, both, preferred_element_type=jnp.float32)
            product = lax.dot_general(value, grad, both, preferred_element_type=jnp.float32)
            fine_bias = fine[...]
            scores = [
                raw[e * TILE : (e + 1) * TILE, :] * SCALE + (fine_bias + entry_bias[e : e + 1, :])
                for e in range(ENTRIES)
            ]
            attend_grad = [product[e * TILE : (e + 1) * TILE, :] for e in range(ENTRIES)]
            top = scores[0]
            for e in range(1, ENTRIES):
                top = jnp.maximum(top, scores[e])
            top = jnp.max(top, axis=0, keepdims=True)
            expo = [jnp.exp(block - top) for block in scores]
            total, weighted = expo[0], expo[0] * attend_grad[0]
            for e in range(1, ENTRIES):
                total = total + expo[e]
                weighted = weighted + expo[e] * attend_grad[e]
            inverse = 1.0 / jnp.sum(total, axis=0, keepdims=True)
            delta = jnp.sum(weighted, axis=0, keepdims=True) * inverse
            attend = [block * inverse for block in expo]
            score_grad = [attend[e] * (attend_grad[e] - delta) for e in range(ENTRIES)]
            attend_low = jnp.concatenate([b.astype(jnp.bfloat16) for b in attend], axis=0)
            grad_low = jnp.concatenate([b.astype(jnp.bfloat16) for b in score_grad], axis=0)
            value_part[q] = jnp.dot(attend_low, grad, preferred_element_type=jnp.float32)
            key_part[q] = jnp.dot(grad_low, query, preferred_element_type=jnp.float32) * SCALE
            query_grad = lax.dot_general(
                key, grad_low, (((0,), (0,)), ((), ())), preferred_element_type=jnp.float32
            )
            ret[c, 0, q] = (query_grad.T * SCALE).astype(jnp.bfloat16)
            total_grad = score_grad[0]
            for e in range(1, ENTRIES):
                total_grad = total_grad + score_grad[e]
            fine_sum[...] += total_grad[:, 0:TILE] + total_grad[:, TILE : 2 * TILE]
            coarse = jnp.zeros((1, TABLE), jnp.float32)
            for e in range(ENTRIES):
                block_sum = jnp.sum(score_grad[e], axis=0, keepdims=True)
                coarse = coarse + jnp.sum(block_sum, axis=1, keepdims=True) * hot[e : e + 1, :]
            coarse_sum[0:1, :] += coarse
            return carry

        lax.fori_loop(0, SIDE, one_query_tile, 0)
        for j in ORDER:
            give_back(0, c, j)
        parts = (key_part, value_part)

        def return_far(c, a, j):
            tile = lax.rem(x + j, SIDE)
            at = (ENTRIES - 1) * TILE
            backs[2][c, a, tile] = parts[a][tile, at : at + TILE, :].astype(jnp.bfloat16)
            far_back(c, a, tile).start()

        for a in range(2):
            for g, (group, _) in enumerate(GROUPS[:2]):
                for n, (q, s, _) in enumerate(group):
                    at = (TILES_DEV + s) * TILE
                    backs[g][c, a, n] = parts[a][q, at : at + TILE, :].astype(jnp.bfloat16)
                back_copy(g, c, a).start()
            for j in ORDER[:-1]:
                return_far(c, a, j)
        for a in range(2):
            return_far(c, a, 0)
        slot = lax.rem(c, 2)
        for a in range(2):
            for q in range(SIDE):
                acc[slot, a, q] = parts[a][q, 0 : 2 * TILE, :]
            for q, s, tile in LOCAL:
                at = (TILES_DEV + s) * TILE
                deposit(slot, a, tile, upper(y, q, s), parts[a][q, at : at + TILE, :])

        folded = fine_sum[...].reshape(TILE_ROWS, TILE_COLS, TILE)
        across = (((1,), (1,)), ((), ()))
        column_grad = lax.dot_general(
            jnp.sum(folded, axis=0), column_hot, across, precision=HIGHEST,
            preferred_element_type=jnp.float32,
        )
        row_grad = lax.dot_general(
            jnp.sum(folded, axis=1), row_hot, across, precision=HIGHEST,
            preferred_element_type=jnp.float32,
        )
        table_row = coarse_sum[0:1, :]
        for j in range(TILE_COLS):
            table_row = table_row + pltpu.roll(column_grad[j : j + 1, :], BUCKETS + j, 1)
        for j in range(TILE_ROWS):
            table_row = table_row + pltpu.roll(
                row_grad[j : j + 1, :], BUCKETS + COLUMN_WIDTH + j, 1
            )
        grads[pl.ds(c, 1), :] = table_row

    def deposit(slot, a, tile, pick, partial):
        acc[slot, a, tile, 0:TILE, :] += jnp.where(pick, 0.0, partial)
        acc[slot, a, tile, TILE : 2 * TILE, :] += jnp.where(pick, partial, 0.0)

    def finish_tile(c, a, j):
        slot = lax.rem(c, 2)
        tile = lax.rem(x + j, SIDE)
        arrived(homes[2].at[c, a, tile], far_recv.at[c, a, tile])
        deposit(
            slot, a, tile, upper(y + SIDE // 2, tile, SLOTS - 1),
            homes[2][c, a, tile].astype(jnp.float32),
        )
        ret[c, 1 + a, tile] = acc[slot, a, tile].astype(jnp.bfloat16)
        give_back(1 + a, c, j)

    def finish(c):
        slot = lax.rem(c, 2)
        for a in range(2):
            for g, (group, distance) in enumerate(GROUPS[:2]):
                arrived(homes[g].at[c, a], home_recv.at[c, g, a])
                for n, (q, s, tile) in enumerate(group):
                    deposit(
                        slot, a, tile, upper(y + distance, q, s),
                        homes[g][c, a, n].astype(jnp.float32),
                    )
            for j in ORDER[:-1]:
                finish_tile(c, a, j)
        for a in range(2):
            finish_tile(c, a, 0)

    def dp_copy(j):
        return remote(
            grads, grads_dp.at[part], dp_send.at[j], dp_recv.at[part],
            {"dp": lax.rem(part + j, DP)},
        )

    def seq_copy(j):
        return remote(
            grads_seq.at[place], grads_seq.at[place], seq_send.at[j], seq_recv.at[place],
            {"seq": lax.rem(place + j, SEQ)},
        )

    def step(t, carry):
        @pl.when(t < CHUNKS)
        def _():
            send_tiles(t)

        @pl.when(t == 1)
        def _():
            for j in range(1, DP):
                source = lax.rem(part + j, DP)
                arrived(tables.at[source], table_recv.at[source])
            for j in range(1, SIDE):
                source = lax.rem(x + j, SIDE)
                arrived(entries.at[source], entry_recv.at[source])

        @pl.when(t >= 2)
        def _():
            compute(t - 2)

        @pl.when(t == CHUNKS + 1)
        def _():
            for j in range(1, DP):
                dp_copy(j).start()

        @pl.when(t >= 3)
        def _():
            finish(t - 3)

        return carry

    lax.fori_loop(0, CHUNKS + 2, step, 0)

    total = grads[...]
    for j in range(1, DP):
        source = lax.rem(part + j, DP)
        arrived(grads_dp.at[source], dp_recv.at[source])
        total = total + grads_dp[source]
    grads_seq[place] = total
    for j in range(1, SEQ):
        seq_copy(j).start()
    finish(CHUNKS - 1)
    for j in range(1, SEQ):
        source = lax.rem(place + j, SEQ)
        arrived(grads_seq.at[source], seq_recv.at[source])
    owner = lax.div(part, 2)
    mine = grads_seq[owner]
    for j in range(1, SIDE):
        mine = mine + grads_seq[owner + j * SIDE]
    own = HEADS // DP
    table_out[...] = jnp.where(lax.rem(part, 2) == 0, mine[0:own, :], mine[own : 2 * own, :])

    peers = slice(0, SIDE - 1)
    arrived(kv_in.at[:, :, peers], kv_send)
    arrived(qd_in.at[:, :, peers], qd_send)
    for g in range(3):
        arrived(gives[g], give_send.at[g])
        arrived(backs[g], back_send.at[g])
    for a in range(3):
        arrived(ret.at[:, a, peers], ret_send.at[a])
    for j in range(1, DP):
        table_copy(j).wait_send()
        dp_copy(j).wait_send()
    for j in range(1, SIDE):
        entry_copy(j).wait_send()
    for j in range(1, SEQ):
        seq_copy(j).wait_send()
    for a in range(3):
        arrived(outs[a], out_recv.at[a])


def per_device(queries, keys, values, grad_out, bias_table, slot_tiles, live, buckets):
    hbm = pl.BlockSpec(memory_space=pltpu.HBM)
    vmem = pl.BlockSpec(memory_space=pltpu.VMEM)
    low, full = jnp.bfloat16, jnp.float32
    dma = pltpu.SemaphoreType.DMA
    moved = [pltpu.VMEM((CHUNKS, 2, len(group), TILE, HEAD_DIM), low) for group, _ in GROUPS]
    set_rows = ENTRIES * TILE
    out = jax.ShapeDtypeStruct((TOK_DEV, WIDTH), low)
    result = pl.pallas_call(
        kernel,
        out_shape=(out, out, out, jax.ShapeDtypeStruct((HEADS // DP, TABLE), full)),
        in_specs=[hbm] * 4 + [vmem, hbm, hbm, hbm],
        out_specs=(hbm, hbm, hbm, vmem),
        scratch_shapes=[
            pltpu.VMEM((CHUNKS, 2, SIDE, TOK_DEV, HEAD_DIM), low),
            pltpu.VMEM((CHUNKS, 2, SIDE, TOK_DEV, HEAD_DIM), low),
            *moved, *moved, *moved, *moved,
            pltpu.VMEM((CHUNKS, 3, SIDE, TOK_DEV, HEAD_DIM), low),
            pltpu.VMEM((2, 2, SIDE, TOK_DEV, HEAD_DIM), full),
            pltpu.VMEM((SIDE, set_rows, HEAD_DIM), low),
            pltpu.VMEM((SIDE, set_rows, HEAD_DIM), low),
            pltpu.VMEM((SIDE, set_rows, HEAD_DIM), full),
            pltpu.VMEM((SIDE, set_rows, HEAD_DIM), full),
            pltpu.SMEM((SLOTS, SEQ), jnp.int32),
            pltpu.SMEM(live.shape, jnp.int32),
            pltpu.SMEM(buckets.shape, jnp.int32),
            pltpu.VMEM((2, SIDE, TOK_DEV, HEAD_DIM), low),
            pltpu.VMEM((2, SIDE, TILE, HEAD_DIM), low),
            pltpu.VMEM((2, CHUNKS - 1, TOK_DEV, HEAD_DIM), low),
            pltpu.VMEM((2, CHUNKS - 1, TILE, HEAD_DIM), low),
            pltpu.VMEM((DP, 8, TABLE), full),
            pltpu.VMEM((SIDE, 2, 8, TABLE), full),
            pltpu.VMEM((TILE_COLS + TILE_ROWS, TABLE), full),
            pltpu.VMEM((TILE, 2 * TILE), full),
            pltpu.VMEM((TILE, TILE), full),
            pltpu.VMEM((8, TABLE), full),
            pltpu.VMEM((8, TABLE), full),
            pltpu.VMEM((DP, 8, TABLE), full),
            pltpu.VMEM((SEQ, 8, TABLE), full),
            dma((3,)), dma(()), dma(()),
            dma(()), dma((CHUNKS, 2)),
            dma(()), dma((CHUNKS, 2)),
            dma((3,)), dma((CHUNKS, 3, 2)),
            dma((3,)), dma((CHUNKS, 2, 2)), dma((CHUNKS, 2, SIDE)),
            dma((3,)), dma((3,)),
            dma((DP,)), dma((DP,)),
            dma((SIDE,)), dma((SIDE,)),
            dma((DP,)), dma((DP,)),
            dma((SEQ,)), dma((SEQ,)),
        ],
        compiler_params=pltpu.CompilerParams(
            collective_id=0, has_side_effects=True, vmem_limit_bytes=60 * 2**20
        ),
        cost_estimate=pl.CostEstimate(
            flops=7_046_430_720, bytes_accessed=11_000_000, transcendentals=5_505_024
        ),
    )(queries[0], keys[0], values[0], grad_out[0], bias_table, slot_tiles.T, live, buckets)
    query_grad, key_grad, value_grad, table_grad = result
    return (query_grad[None], key_grad[None], value_grad[None], table_grad)


def solution(mesh):
    rows = P("dp", "seq", None)
    return jax.shard_map(
        per_device,
        mesh=mesh,
        in_specs=(rows, rows, rows, rows, P("dp", None), P(), P("seq", None), P("seq", None)),
        out_specs=(rows, rows, rows, P("dp", None)),
        check_vma=False,
    )
```

```python
import jax
import jax.numpy as jnp
from jax import lax
from jax.experimental import pallas as pl
from jax.experimental.pallas import tpu as pltpu
from jax.sharding import PartitionSpec as P

HEADS = 24
HEAD_DIM = 128
TOK_DEV = 256
TILE = 128
TILE_COLS = 16
TILE_ROWS = TILE // TILE_COLS
SLOTS = 5
BUCKETS = 82
WIDTH = 3072
TILES_DEV = 2
ENTRIES = TILES_DEV + SLOTS
COLUMN_WIDTH = 2 * TILE_COLS - 1
TABLE = 128

SIDE = 4
SEQ = SIDE * SIDE
DP = 8
STRIDES = (1, 2, 4)
CHUNKS = HEADS // SIDE
NEGATIVE = -1e30
SCALE = HEAD_DIM ** (-0.5)
NEAR_OFFSETS = (-1, 1, -2, 2)
HIGHEST = lax.Precision.HIGHEST
MESH = pl.DeviceIdType.MESH

ORDER = (2, 1, 3, 0)

FROM_BELOW = tuple((q, s, q + o + SIDE) for q in range(SIDE) for s, o in enumerate(NEAR_OFFSETS) if q + o < 0)
FROM_ABOVE = tuple((q, s, q + o - SIDE) for q in range(SIDE) for s, o in enumerate(NEAR_OFFSETS) if q + o >= SIDE)
FROM_HALF = tuple((q, SLOTS - 1, q) for q in range(SIDE))
GROUPS = ((FROM_BELOW, 1), (FROM_ABOVE, SIDE - 1), (FROM_HALF, SIDE // 2))
LOCAL = tuple(
    (q, s, q + o) for q in range(SIDE) for s, o in enumerate(NEAR_OFFSETS) if 0 <= q + o < SIDE
)


def iota(shape, axis):
    return lax.broadcasted_iota(jnp.int32, shape, axis)


def kernel(
    queries, keys, values, upstream, table_hbm, slots_hbm, live_hbm, buckets_hbm,
    query_out, key_out, value_out, table_out,
    kv_in, qd_in, give0, give1, give2, got0, got1, got2, back0, back1, back2, home0, home1, home2,
    ret, acc, key_set, value_set, key_part, value_part,
    table, slots, live, buckets, own_heads, own_far,
    tables, entries, shifted, fine, fine_sum, coarse_sum, grads, grads_dp, grads_seq,
    small_recv, own_recv,
    kv_send, kv_recv, qd_send, qd_recv, give_send, got_recv, back_send, home_recv, far_recv, ret_send, out_recv,
    table_send, table_recv, entry_send, entry_recv, dp_send, dp_recv, seq_send, seq_recv,
):
    gives, gots = (give0, give1, give2), (got0, got1, got2)
    backs, homes = (back0, back1, back2), (home0, home1, home2)
    outs = (query_out, key_out, value_out)
    place = lax.axis_index("seq")
    part = lax.axis_index("dp")
    x, y = lax.rem(place, SIDE), lax.div(place, SIDE)

    def seq_at(column, row):
        return {"seq": lax.rem(row, SIDE) * SIDE + lax.rem(column, SIDE)}

    def remote(source, target, send, recv, device):
        return pltpu.make_async_remote_copy(
            src_ref=source, dst_ref=target, send_sem=send, recv_sem=recv,
            device_id=device, device_id_type=MESH,
        )

    def arrived(buffer, semaphore):
        pltpu.make_async_copy(buffer, buffer, semaphore).wait()

    def head_columns(head):
        return pl.ds(pl.multiple_of(head * HEAD_DIM, HEAD_DIM), HEAD_DIM)

    barrier = pltpu.get_barrier_semaphore()
    pairs = tuple(part + o - 2 * o * lax.rem(lax.div(part, o), 2) for o in STRIDES)
    greeted = [seq_at(x + j, y) for j in range(1, SIDE)]
    greeted += [seq_at(x, y + j) for j in range(1, SIDE)]
    greeted += [{"dp": pair} for pair in pairs]
    for device in greeted:
        pl.semaphore_signal(barrier, inc=1, device_id=device, device_id_type=MESH)
    small = [
        pltpu.make_async_copy(source, target, small_recv.at[n])
        for n, (source, target) in enumerate(
            ((slots_hbm, slots), (live_hbm, live), (buckets_hbm, buckets), (table_hbm, table))
        )
    ]
    for copy in small:
        copy.start()
    for a, ref in enumerate((keys, values)):
        for c in range(CHUNKS):
            pltpu.make_async_copy(
                ref.at[:, head_columns(x * CHUNKS + c)], own_heads.at[a, c], own_recv
            ).start()
    for copy in small:
        copy.wait()

    def upper(query_row, q, s):
        return lax.rem(slots[s, lax.rem(query_row, SIDE) * SIDE + q], TILES_DEV) == 1

    lane = iota((8, TABLE), 1)
    row = iota((8, TABLE), 0)
    tables[part] = jnp.zeros((8, TABLE), jnp.float32)
    tables[part, 0 : HEADS // DP, :] = table[...]
    bucket = jnp.full((8, TABLE), -1, jnp.int32)
    alive = jnp.zeros((8, TABLE), jnp.int32)
    for e in range(ENTRIES):
        bucket = jnp.where(row == e, buckets[0, e], bucket)
        alive = jnp.where(row == e, live[0, e], alive)
    entries[x, 0] = (lane == bucket).astype(jnp.float32)
    entries[x, 1] = jnp.where(alive > 0, 0.0, NEGATIVE)
    grads[...] = jnp.zeros_like(grads)
    arrived(own_heads, own_recv)
    half_pick = upper(y + SIDE // 2, x, SLOTS - 1)
    for a in range(2):
        for c in range(CHUNKS):
            own_far[a, c] = jnp.where(
                half_pick, own_heads[a, c, TILE : 2 * TILE, :], own_heads[a, c, 0:TILE, :]
            )

    pl.semaphore_wait(barrier, len(greeted))

    def table_block(device, n):
        stride = STRIDES[n]
        return tables.at[pl.ds(lax.div(device, stride) * stride, stride)]

    def table_copy(n):
        block = table_block(part, n)
        return remote(block, block, table_send.at[n], table_recv.at[n], {"dp": pairs[n]})

    def table_arrived(n):
        arrived(table_block(pairs[n], n), table_recv.at[n])

    def entry_copy(j):
        return remote(
            entries.at[x], entries.at[x], entry_send.at[j], entry_recv.at[x], seq_at(x + j, y)
        )

    def fetch(refs, buffer, send, recv, c):
        for a, ref in enumerate(refs):
            for j in ORDER[:-1]:
                to = lax.rem(x + j, SIDE)
                remote(
                    ref.at[:, head_columns(to * CHUNKS + c)], buffer.at[c, a, x],
                    send, recv.at[c, a], seq_at(to, y),
                ).start()
            pltpu.make_async_copy(
                ref.at[:, head_columns(x * CHUNKS + c)], buffer.at[c, a, x], recv.at[c, a]
            ).start()

    kv = ((keys, values), kv_in, kv_send, kv_recv)
    qd = ((queries, upstream), qd_in, qd_send, qd_recv)

    def give_copy(g, c, a):
        return remote(
            gives[g].at[c, a], gots[g].at[c, a], give_send.at[g], got_recv.at[c, g, a],
            seq_at(x, y + GROUPS[g][1]),
        )

    def back_copy(g, c, a):
        return remote(
            backs[g].at[c, a], homes[g].at[c, a], back_send.at[g], home_recv.at[c, g, a],
            seq_at(x, y + SIDE - GROUPS[g][1]),
        )

    def far_back(c, a, tile):
        return remote(
            backs[2].at[c, a, tile], homes[2].at[c, a, tile], back_send.at[2],
            far_recv.at[c, a, tile], seq_at(x, y + SIDE // 2),
        )

    def give_back(a, c, j):
        columns = head_columns(x * CHUNKS + c)
        source = ret.at[c, a, lax.rem(x + j, SIDE)]
        if j == 0:
            pltpu.make_async_copy(source, outs[a].at[:, columns], out_recv.at[a]).start()
        else:
            remote(
                source, outs[a].at[:, columns], ret_send.at[a], out_recv.at[a], seq_at(x + j, y)
            ).start()

    table_copy(0).start()
    for j in range(1, SIDE):
        entry_copy(j).start()
    for c in range(CHUNKS):
        for a in range(2):
            remote(
                own_far.at[a, c], gots[2].at[c, a, x], give_send.at[2], got_recv.at[c, 2, a],
                seq_at(x, y + SIDE // 2),
            ).start()
        if c == 0:
            fetch(*kv, 0)
    fetch(*kv, 1)
    fetch(*kv, 2)
    fetch(*qd, 0)
    table_arrived(0)
    table_copy(1).start()

    def halves(c, a, tile):
        return kv_in[c, a, tile, 0:TILE, :], kv_in[c, a, tile, TILE : 2 * TILE, :]

    def send_tiles(c):
        for a in range(2):
            arrived(kv_in.at[c, a], kv_recv.at[c, a])
            for g, (group, distance) in enumerate(GROUPS[:2]):
                for n, (q, s, tile) in enumerate(group):
                    low, high = halves(c, a, tile)
                    gives[g][c, a, n] = jnp.where(upper(y + distance, q, s), high, low)
                give_copy(g, c, a).start()

            for j in ORDER[:-1]:
                tile = lax.rem(x + j, SIDE)
                low, high = halves(c, a, tile)
                pick = upper(y + SIDE // 2, tile, SLOTS - 1)
                gives[2][c, a, tile] = jnp.where(pick, high, low)
                remote(
                    gives[2].at[c, a, tile], gots[2].at[c, a, tile], give_send.at[2],
                    got_recv.at[c, 2, a], seq_at(x, y + SIDE // 2),
                ).start()

        @pl.when(c + 3 < CHUNKS)
        def _():
            fetch(*kv, c + 3)

        @pl.when(c + 1 < CHUNKS)
        def _():
            fetch(*qd, c + 1)

    def compute(c):
        for a in range(2):
            arrived(qd_in.at[c, a], qd_recv.at[c, a])
            for g in range(3):
                arrived(gots[g].at[c, a], got_recv.at[c, g, a])
        sets = (key_set, value_set)
        for a in range(2):
            for q in range(SIDE):
                sets[a][q, 0 : 2 * TILE, :] = kv_in[c, a, q]
            for q, s, tile in LOCAL:
                low, high = halves(c, a, tile)
                at = (TILES_DEV + s) * TILE
                sets[a][q, at : at + TILE, :] = jnp.where(upper(y, q, s), high, low)
            for g, (group, _) in enumerate(GROUPS):
                for n, (q, s, _) in enumerate(group):
                    at = (TILES_DEV + s) * TILE
                    sets[a][q, at : at + TILE, :] = gots[g][c, a, n]

        head_row = tables[2 * x + lax.div(c, 3), pl.ds(lax.rem(c, 3), 1), :]
        for j in range(TILE_COLS):
            shifted[j : j + 1, :] = pltpu.roll(head_row, (2 * TABLE - BUCKETS - j) % TABLE, 1)
        for j in range(TILE_ROWS):
            shifted[TILE_COLS + j : TILE_COLS + j + 1, :] = pltpu.roll(
                head_row, (2 * TABLE - BUCKETS - COLUMN_WIDTH - j) % TABLE, 1
            )
        offset = iota((TABLE, TILE), 0)
        query_at = iota((TABLE, TILE), 1)
        column_hot = (offset == TILE_COLS - 1 - lax.rem(query_at, TILE_COLS)).astype(jnp.float32)
        row_hot = (offset == TILE_ROWS - 1 - lax.div(query_at, TILE_COLS)).astype(jnp.float32)
        column_bias = jnp.dot(
            shifted[0:TILE_COLS, :], column_hot, precision=HIGHEST,
            preferred_element_type=jnp.float32,
        )
        row_bias = jnp.dot(
            shifted[TILE_COLS : TILE_COLS + TILE_ROWS, :], row_hot, precision=HIGHEST,
            preferred_element_type=jnp.float32,
        )
        for j in range(TILE_ROWS):
            band = column_bias + row_bias[j : j + 1, :]
            fine[j * TILE_COLS : (j + 1) * TILE_COLS, 0:TILE] = band
            fine[j * TILE_COLS : (j + 1) * TILE_COLS, TILE : 2 * TILE] = band
        fine_sum[...] = jnp.zeros_like(fine_sum)
        coarse_sum[...] = jnp.zeros_like(coarse_sum)

        def one_query_tile(q, carry):
            query = qd_in[c, 0, q]
            grad = qd_in[c, 1, q]
            key = key_set[q]
            value = value_set[q]
            hot = entries[q, 0]
            entry_bias = jnp.sum(hot * head_row, axis=1, keepdims=True) + entries[q, 1][:, 0:1]
            both = (((1,), (1,)), ((), ()))
            raw = lax.dot_general(key, query, both, preferred_element_type=jnp.float32)
            product = lax.dot_general(value, grad, both, preferred_element_type=jnp.float32)
            fine_bias = fine[...]
            scores = [
                raw[e * TILE : (e + 1) * TILE, :] * SCALE + (fine_bias + entry_bias[e : e + 1, :])
                for e in range(ENTRIES)
            ]
            attend_grad = [product[e * TILE : (e + 1) * TILE, :] for e in range(ENTRIES)]
            top = scores[0]
            for e in range(1, ENTRIES):
                top = jnp.maximum(top, scores[e])
            top = jnp.max(top, axis=0, keepdims=True)
            expo = [jnp.exp(block - top) for block in scores]
            total, weighted = expo[0], expo[0] * attend_grad[0]
            for e in range(1, ENTRIES):
                total = total + expo[e]
                weighted = weighted + expo[e] * attend_grad[e]
            inverse = 1.0 / jnp.sum(total, axis=0, keepdims=True)
            delta = jnp.sum(weighted, axis=0, keepdims=True) * inverse
            attend = [block * inverse for block in expo]
            score_grad = [attend[e] * (attend_grad[e] - delta) for e in range(ENTRIES)]
            attend_low = jnp.concatenate([b.astype(jnp.bfloat16) for b in attend], axis=0)
            grad_low = jnp.concatenate([b.astype(jnp.bfloat16) for b in score_grad], axis=0)
            value_part[q] = jnp.dot(attend_low, grad, preferred_element_type=jnp.float32)
            key_part[q] = jnp.dot(grad_low, query, preferred_element_type=jnp.float32) * SCALE
            query_grad = lax.dot_general(
                key, grad_low, (((0,), (0,)), ((), ())), preferred_element_type=jnp.float32
            )
            ret[c, 0, q] = (query_grad.T * SCALE).astype(jnp.bfloat16)
            total_grad = score_grad[0]
            for e in range(1, ENTRIES):
                total_grad = total_grad + score_grad[e]
            fine_sum[...] += total_grad[:, 0:TILE] + total_grad[:, TILE : 2 * TILE]
            coarse = jnp.zeros((1, TABLE), jnp.float32)
            for e in range(ENTRIES):
                block_sum = jnp.sum(score_grad[e], axis=0, keepdims=True)
                coarse = coarse + jnp.sum(block_sum, axis=1, keepdims=True) * hot[e : e + 1, :]
            coarse_sum[0:1, :] += coarse
            return carry

        lax.fori_loop(0, SIDE, one_query_tile, 0)
        for j in ORDER:
            give_back(0, c, j)
        parts = (key_part, value_part)

        def return_far(c, a, j):
            tile = lax.rem(x + j, SIDE)
            at = (ENTRIES - 1) * TILE
            backs[2][c, a, tile] = parts[a][tile, at : at + TILE, :].astype(jnp.bfloat16)
            far_back(c, a, tile).start()

        for a in range(2):
            for g, (group, _) in enumerate(GROUPS[:2]):
                for n, (q, s, _) in enumerate(group):
                    at = (TILES_DEV + s) * TILE
                    backs[g][c, a, n] = parts[a][q, at : at + TILE, :].astype(jnp.bfloat16)
                back_copy(g, c, a).start()
            for j in ORDER[:-1]:
                return_far(c, a, j)
        for a in range(2):
            return_far(c, a, 0)
        slot = lax.rem(c, 2)
        for a in range(2):
            for q in range(SIDE):
                acc[slot, a, q] = parts[a][q, 0 : 2 * TILE, :]
            for q, s, tile in LOCAL:
                at = (TILES_DEV + s) * TILE
                deposit(slot, a, tile, upper(y, q, s), parts[a][q, at : at + TILE, :])

        folded = fine_sum[...].reshape(TILE_ROWS, TILE_COLS, TILE)
        across = (((1,), (1,)), ((), ()))
        column_grad = lax.dot_general(
            jnp.sum(folded, axis=0), column_hot, across, precision=HIGHEST,
            preferred_element_type=jnp.float32,
        )
        row_grad = lax.dot_general(
            jnp.sum(folded, axis=1), row_hot, across, precision=HIGHEST,
            preferred_element_type=jnp.float32,
        )
        table_row = coarse_sum[0:1, :]
        for j in range(TILE_COLS):
            table_row = table_row + pltpu.roll(column_grad[j : j + 1, :], BUCKETS + j, 1)
        for j in range(TILE_ROWS):
            table_row = table_row + pltpu.roll(
                row_grad[j : j + 1, :], BUCKETS + COLUMN_WIDTH + j, 1
            )
        grads[pl.ds(c, 1), :] = table_row

    def deposit(slot, a, tile, pick, partial):
        acc[slot, a, tile, 0:TILE, :] += jnp.where(pick, 0.0, partial)
        acc[slot, a, tile, TILE : 2 * TILE, :] += jnp.where(pick, partial, 0.0)

    def finish_tile(c, a, j):
        slot = lax.rem(c, 2)
        tile = lax.rem(x + j, SIDE)
        arrived(homes[2].at[c, a, tile], far_recv.at[c, a, tile])
        deposit(
            slot, a, tile, upper(y + SIDE // 2, tile, SLOTS - 1),
            homes[2][c, a, tile].astype(jnp.float32),
        )
        ret[c, 1 + a, tile] = acc[slot, a, tile].astype(jnp.bfloat16)
        give_back(1 + a, c, j)

    def finish(c):
        slot = lax.rem(c, 2)
        for a in range(2):
            for g, (group, distance) in enumerate(GROUPS[:2]):
                arrived(homes[g].at[c, a], home_recv.at[c, g, a])
                for n, (q, s, tile) in enumerate(group):
                    deposit(
                        slot, a, tile, upper(y + distance, q, s),
                        homes[g][c, a, n].astype(jnp.float32),
                    )
            for j in ORDER[:-1]:
                finish_tile(c, a, j)
        for a in range(2):
            finish_tile(c, a, 0)

    def dp_copy(j):
        return remote(
            grads, grads_dp.at[part], dp_send.at[j], dp_recv.at[part],
            {"dp": lax.rem(part + j, DP)},
        )

    def seq_copy(j):
        return remote(
            grads_seq.at[place], grads_seq.at[place], seq_send.at[j], seq_recv.at[place],
            {"seq": lax.rem(place + j, SEQ)},
        )

    def step(t, carry):
        @pl.when(t < CHUNKS)
        def _():
            send_tiles(t)

        @pl.when(t == 1)
        def _():
            table_arrived(1)
            table_copy(2).start()
            for j in range(1, SIDE):
                source = lax.rem(x + j, SIDE)
                arrived(entries.at[source], entry_recv.at[source])

        @pl.when(t == 2)
        def _():
            table_arrived(2)

        @pl.when(t >= 2)
        def _():
            compute(t - 2)

        @pl.when(t == CHUNKS + 1)
        def _():
            for j in range(1, DP):
                dp_copy(j).start()

        @pl.when(t >= 3)
        def _():
            finish(t - 3)

        return carry

    lax.fori_loop(0, CHUNKS + 2, step, 0)

    total = grads[...]
    for j in range(1, DP):
        source = lax.rem(part + j, DP)
        arrived(grads_dp.at[source], dp_recv.at[source])
        total = total + grads_dp[source]
    grads_seq[place] = total
    for j in range(1, SEQ):
        seq_copy(j).start()
    finish(CHUNKS - 1)
    for j in range(1, SEQ):
        source = lax.rem(place + j, SEQ)
        arrived(grads_seq.at[source], seq_recv.at[source])
    owner = lax.div(part, 2)
    mine = grads_seq[owner]
    for j in range(1, SIDE):
        mine = mine + grads_seq[owner + j * SIDE]
    own = HEADS // DP
    table_out[...] = jnp.where(lax.rem(part, 2) == 0, mine[0:own, :], mine[own : 2 * own, :])

    peers = slice(0, SIDE - 1)
    arrived(kv_in.at[:, :, peers], kv_send)
    arrived(qd_in.at[:, :, peers], qd_send)
    for g in range(3):
        arrived(gives[g], give_send.at[g])
        arrived(backs[g], back_send.at[g])
    for a in range(3):
        arrived(ret.at[:, a, peers], ret_send.at[a])
    for n in range(len(STRIDES)):
        table_copy(n).wait_send()
    for j in range(1, DP):
        dp_copy(j).wait_send()
    for j in range(1, SIDE):
        entry_copy(j).wait_send()
    for j in range(1, SEQ):
        seq_copy(j).wait_send()
    for a in range(3):
        arrived(outs[a], out_recv.at[a])


def per_device(queries, keys, values, grad_out, bias_table, slot_tiles, live, buckets):
    hbm = pl.BlockSpec(memory_space=pltpu.HBM)
    vmem = pl.BlockSpec(memory_space=pltpu.VMEM)
    low, full = jnp.bfloat16, jnp.float32
    dma = pltpu.SemaphoreType.DMA
    moved = [pltpu.VMEM((CHUNKS, 2, len(group), TILE, HEAD_DIM), low) for group, _ in GROUPS]
    set_rows = ENTRIES * TILE
    out = pltpu.VMEM((TOK_DEV, WIDTH), low)
    operands = (
        queries[0], keys[0], values[0], grad_out[0], bias_table, slot_tiles.T, live, buckets,
    )
    result = pl.pallas_call(
        kernel,
        out_shape=(out, out, out, jax.ShapeDtypeStruct((HEADS // DP, TABLE), full)),
        in_specs=[hbm] * len(operands),
        out_specs=(vmem, vmem, vmem, vmem),
        scratch_shapes=[
            pltpu.VMEM((CHUNKS, 2, SIDE, TOK_DEV, HEAD_DIM), low),
            pltpu.VMEM((CHUNKS, 2, SIDE, TOK_DEV, HEAD_DIM), low),
            *moved, *moved, *moved, *moved,
            pltpu.VMEM((CHUNKS, 3, SIDE, TOK_DEV, HEAD_DIM), low),
            pltpu.VMEM((2, 2, SIDE, TOK_DEV, HEAD_DIM), full),
            pltpu.VMEM((SIDE, set_rows, HEAD_DIM), low),
            pltpu.VMEM((SIDE, set_rows, HEAD_DIM), low),
            pltpu.VMEM((SIDE, set_rows, HEAD_DIM), full),
            pltpu.VMEM((SIDE, set_rows, HEAD_DIM), full),
            pltpu.VMEM(bias_table.shape, full),
            pltpu.SMEM((SLOTS, SEQ), jnp.int32),
            pltpu.SMEM(live.shape, jnp.int32),
            pltpu.SMEM(buckets.shape, jnp.int32),
            pltpu.VMEM((2, CHUNKS, TOK_DEV, HEAD_DIM), low),
            pltpu.VMEM((2, CHUNKS, TILE, HEAD_DIM), low),
            pltpu.VMEM((DP, 8, TABLE), full),
            pltpu.VMEM((SIDE, 2, 8, TABLE), full),
            pltpu.VMEM((TILE_COLS + TILE_ROWS, TABLE), full),
            pltpu.VMEM((TILE, 2 * TILE), full),
            pltpu.VMEM((TILE, TILE), full),
            pltpu.VMEM((8, TABLE), full),
            pltpu.VMEM((8, TABLE), full),
            pltpu.VMEM((DP, 8, TABLE), full),
            pltpu.VMEM((SEQ, 8, TABLE), full),
            dma((4,)), dma(()),
            dma(()), dma((CHUNKS, 2)),
            dma(()), dma((CHUNKS, 2)),
            dma((3,)), dma((CHUNKS, 3, 2)),
            dma((3,)), dma((CHUNKS, 2, 2)), dma((CHUNKS, 2, SIDE)),
            dma((3,)), dma((3,)),
            dma((len(STRIDES),)), dma((len(STRIDES),)),
            dma((SIDE,)), dma((SIDE,)),
            dma((DP,)), dma((DP,)),
            dma((SEQ,)), dma((SEQ,)),
        ],
        compiler_params=pltpu.CompilerParams(
            collective_id=0, has_side_effects=True, vmem_limit_bytes=48 * 2**20
        ),
        cost_estimate=pl.CostEstimate(
            flops=7_046_430_720, bytes_accessed=11_000_000, transcendentals=5_505_024
        ),
    )(*[pltpu.with_memory_space_constraint(operand, pltpu.HBM) for operand in operands])
    query_grad, key_grad, value_grad, table_grad = result
    return (query_grad[None], key_grad[None], value_grad[None], table_grad)


def solution(mesh):
    rows = P("dp", "seq", None)
    return jax.shard_map(
        per_device,
        mesh=mesh,
        in_specs=(rows, rows, rows, rows, P("dp", None), P(), P("seq", None), P("seq", None)),
        out_specs=(rows, rows, rows, P("dp", None)),
        check_vma=False,
    )
```

```python
import jax
import jax.numpy as jnp
from jax import lax
from jax.experimental import pallas as pl
from jax.experimental.pallas import tpu as pltpu
from jax.sharding import PartitionSpec as P

HEADS = 24
HEAD_DIM = 128
TOK_DEV = 256
TILE = 128
TILE_COLS = 16
TILE_ROWS = TILE // TILE_COLS
SLOTS = 5
BUCKETS = 82
WIDTH = 3072
TILES_DEV = 2
ENTRIES = TILES_DEV + SLOTS
COLUMN_WIDTH = 2 * TILE_COLS - 1
TABLE = 128

SIDE = 4
SEQ = SIDE * SIDE
DP = 8
STRIDES = (1, 2, 4)
CHUNKS = HEADS // SIDE
NEGATIVE = -1e30
SCALE = HEAD_DIM ** (-0.5)
NEAR_OFFSETS = (-1, 1, -2, 2)
HIGHEST = lax.Precision.HIGHEST
MESH = pl.DeviceIdType.MESH

ORDER = (2, 1, 3, 0)

FROM_BELOW = tuple((q, s, q + o + SIDE) for q in range(SIDE) for s, o in enumerate(NEAR_OFFSETS) if q + o < 0)
FROM_ABOVE = tuple((q, s, q + o - SIDE) for q in range(SIDE) for s, o in enumerate(NEAR_OFFSETS) if q + o >= SIDE)
FROM_HALF = tuple((q, SLOTS - 1, q) for q in range(SIDE))
FIRST = (0, 3, 6, 10)
GROUPS = ((FROM_BELOW, 1), (FROM_ABOVE, SIDE - 1), (FROM_HALF, SIDE // 2))
NEAR = tuple(
    (q, s, tile, 1 + sum(tile == other[2] for other in group[:n]))
    for group in (FROM_BELOW, FROM_ABOVE[::-1])
    for n, (q, s, tile) in enumerate(group)
)
LOCAL = tuple(
    (q, s, q + o) for q in range(SIDE) for s, o in enumerate(NEAR_OFFSETS) if 0 <= q + o < SIDE
)


def iota(shape, axis):
    return lax.broadcasted_iota(jnp.int32, shape, axis)


def kernel(
    queries, keys, values, upstream, table_hbm, slots_hbm, live_hbm, buckets_hbm,
    query_out, key_out, value_out, table_out,
    kv_in, qd_in, give0, give1, give2, got, back, home,
    ret, acc, key_set, value_set, key_part, value_part,
    table, slots, live, buckets, own_heads, own_far,
    tables, entries, shifted, fine, fine_sum, coarse_sum, grads, grads_dp, grads_seq,
    small_recv, own_recv,
    kv_send, kv_recv, qd_send, qd_recv, give_send, got_recv, back_send, home_recv, ret_send, out_recv,
    table_send, table_recv, entry_send, entry_recv, dp_send, dp_recv, seq_send, seq_recv,
):
    gives = (give0, give1, give2)
    outs = (query_out, key_out, value_out)
    place = lax.axis_index("seq")
    part = lax.axis_index("dp")
    x, y = lax.rem(place, SIDE), lax.div(place, SIDE)

    def seq_at(column, row):
        return {"seq": lax.rem(row, SIDE) * SIDE + lax.rem(column, SIDE)}

    def remote(source, target, send, recv, device):
        return pltpu.make_async_remote_copy(
            src_ref=source, dst_ref=target, send_sem=send, recv_sem=recv,
            device_id=device, device_id_type=MESH,
        )

    def arrived(buffer, semaphore):
        pltpu.make_async_copy(buffer, buffer, semaphore).wait()

    peers = slice(0, SIDE - 1)

    def head_columns(head):
        return pl.ds(pl.multiple_of(head * HEAD_DIM, HEAD_DIM), HEAD_DIM)

    barrier = pltpu.get_barrier_semaphore()
    pairs = tuple(part + o - 2 * o * lax.rem(lax.div(part, o), 2) for o in STRIDES)
    greeted = [seq_at(x + j, y) for j in range(1, SIDE)]
    greeted += [seq_at(x, y + j) for j in range(1, SIDE)]
    greeted += [{"dp": pair} for pair in pairs]
    for device in greeted:
        pl.semaphore_signal(barrier, inc=1, device_id=device, device_id_type=MESH)
    small = [
        pltpu.make_async_copy(source, target, small_recv.at[n])
        for n, (source, target) in enumerate(
            ((slots_hbm, slots), (live_hbm, live), (buckets_hbm, buckets), (table_hbm, table))
        )
    ]
    for copy in small:
        copy.start()
    for a, ref in enumerate((keys, values)):
        for c in range(CHUNKS):
            pltpu.make_async_copy(
                ref.at[:, head_columns(x * CHUNKS + c)], own_heads.at[a, c], own_recv
            ).start()
    for copy in small:
        copy.wait()

    def upper(query_row, q, s):
        return lax.rem(slots[s, lax.rem(query_row, SIDE) * SIDE + q], TILES_DEV) == 1

    lane = iota((8, TABLE), 1)
    row = iota((8, TABLE), 0)
    tables[part] = jnp.zeros((8, TABLE), jnp.float32)
    tables[part, 0 : HEADS // DP, :] = table[...]
    bucket = jnp.full((8, TABLE), -1, jnp.int32)
    alive = jnp.zeros((8, TABLE), jnp.int32)
    for e in range(ENTRIES):
        bucket = jnp.where(row == e, buckets[0, e], bucket)
        alive = jnp.where(row == e, live[0, e], alive)
    entries[x, 0] = (lane == bucket).astype(jnp.float32)
    entries[x, 1] = jnp.where(alive > 0, 0.0, NEGATIVE)
    grads[...] = jnp.zeros_like(grads)
    arrived(own_heads, own_recv)
    half_pick = upper(y + SIDE // 2, x, SLOTS - 1)
    for a in range(2):
        for c in range(CHUNKS):
            own_far[a, c] = jnp.where(
                half_pick, own_heads[a, c, TILE : 2 * TILE, :], own_heads[a, c, 0:TILE, :]
            )

    pl.semaphore_wait(barrier, len(greeted))

    def table_block(device, n):
        stride = STRIDES[n]
        return tables.at[pl.ds(lax.div(device, stride) * stride, stride)]

    def table_copy(n):
        block = table_block(part, n)
        return remote(block, block, table_send.at[n], table_recv.at[n], {"dp": pairs[n]})

    def table_arrived(n):
        arrived(table_block(pairs[n], n), table_recv.at[n])

    def entry_copy(j):
        return remote(
            entries.at[x], entries.at[x], entry_send, entry_recv, seq_at(x + j, y)
        )

    def fetch(refs, buffer, send, recvs, c):
        for a, ref in enumerate(refs):
            recv = recvs(c, a)
            for j in ORDER[:-1]:
                to = lax.rem(x + j, SIDE)
                remote(
                    ref.at[:, head_columns(to * CHUNKS + c)], buffer.at[c, a, x],
                    send, recv, seq_at(to, y),
                ).start()
            pltpu.make_async_copy(
                ref.at[:, head_columns(x * CHUNKS + c)], buffer.at[c, a, x], recv
            ).start()

    kv = ((keys, values), kv_in, kv_send, lambda c, a: kv_recv.at[c, a])
    qd = ((queries, upstream), qd_in, qd_send, lambda c, a: qd_recv.at[c])

    def give_copy(g, c, a):
        return remote(
            gives[g].at[c, a], got.at[c, a, FIRST[g] : FIRST[g + 1]], give_send.at[g],
            got_recv.at[c],
            seq_at(x, y + GROUPS[g][1]),
        )

    def back_copy(c, tile, a, n):
        row = SIDE // 2 if n == 0 else jnp.where(tile < 2, 1, SIDE - 1)
        return remote(
            back.at[c, tile, a, n], home.at[c, tile, a, n], back_send, home_recv.at[c, tile],
            seq_at(x, y + row),
        )

    def outer(tile):
        return (tile == 0) | (tile == SIDE - 1)

    def near_pick(tile, n):
        listing_row = y + jnp.where(tile < 2, SIDE - 1, 1)
        if n == 1:
            q = jnp.where(tile < 2, SIDE - 1, 0)
            s = jnp.where(tile == 0, 1, jnp.where(tile == 1, 3, jnp.where(tile == 2, 2, 0)))
        else:
            q = jnp.where(tile == 0, 2, 1)
            s = jnp.where(tile == 0, 3, 2)
        return upper(listing_row, q, s)

    def give_back(a, c, j):
        columns = head_columns(x * CHUNKS + c)
        source = ret.at[c, a, lax.rem(x + j, SIDE)]
        if j == 0:
            outs[a][:, columns] = ret[c, a, x]
        else:
            remote(
                source, outs[a].at[:, columns], ret_send.at[a], out_recv.at[a], seq_at(x + j, y)
            ).start()

    for c in range(CHUNKS):
        for a in range(2):
            remote(
                own_far.at[a, c], got.at[c, a, FIRST[2] + x], give_send.at[2], got_recv.at[c],
                seq_at(x, y + SIDE // 2),
            ).start()
        if c == 0:
            fetch(*kv, 0)
    table_copy(0).start()
    for j in range(1, SIDE):
        entry_copy(j).start()
    fetch(*kv, 1)
    fetch(*kv, 2)
    fetch(*qd, 0)
    table_arrived(0)
    table_copy(1).start()

    def halves(c, a, tile):
        return kv_in[c, a, tile, 0:TILE, :], kv_in[c, a, tile, TILE : 2 * TILE, :]

    def send_tiles(c):
        for a in range(2):
            arrived(kv_in.at[c, a], kv_recv.at[c, a])
            for g, (group, distance) in enumerate(GROUPS[:2]):
                for n, (q, s, tile) in enumerate(group):
                    low, high = halves(c, a, tile)
                    gives[g][c, a, n] = jnp.where(upper(y + distance, q, s), high, low)
                give_copy(g, c, a).start()

            for j in ORDER[:-1]:
                tile = lax.rem(x + j, SIDE)
                low, high = halves(c, a, tile)
                pick = upper(y + SIDE // 2, tile, SLOTS - 1)
                gives[2][c, a, tile] = jnp.where(pick, high, low)
                remote(
                    gives[2].at[c, a, tile], got.at[c, a, FIRST[2] + tile], give_send.at[2],
                    got_recv.at[c], seq_at(x, y + SIDE // 2),
                ).start()

        @pl.when(c + 3 < CHUNKS)
        def _():
            fetch(*kv, c + 3)

        @pl.when(c + 1 < CHUNKS)
        def _():
            fetch(*qd, c + 1)

    def compute(c):
        arrived(qd_in.at[c], qd_recv.at[c])
        arrived(got.at[c], got_recv.at[c])
        sets = (key_set, value_set)
        for a in range(2):
            for q in range(SIDE):
                sets[a][q, 0 : 2 * TILE, :] = kv_in[c, a, q]
            for q, s, tile in LOCAL:
                low, high = halves(c, a, tile)
                at = (TILES_DEV + s) * TILE
                sets[a][q, at : at + TILE, :] = jnp.where(upper(y, q, s), high, low)
            for g, (group, _) in enumerate(GROUPS):
                for n, (q, s, _) in enumerate(group):
                    at = (TILES_DEV + s) * TILE
                    sets[a][q, at : at + TILE, :] = got[c, a, FIRST[g] + n]

        head_row = tables[2 * x + lax.div(c, 3), pl.ds(lax.rem(c, 3), 1), :]
        for j in range(TILE_COLS):
            shifted[j : j + 1, :] = pltpu.roll(head_row, (2 * TABLE - BUCKETS - j) % TABLE, 1)
        for j in range(TILE_ROWS):
            shifted[TILE_COLS + j : TILE_COLS + j + 1, :] = pltpu.roll(
                head_row, (2 * TABLE - BUCKETS - COLUMN_WIDTH - j) % TABLE, 1
            )
        offset = iota((TABLE, TILE), 0)
        query_at = iota((TABLE, TILE), 1)
        column_hot = (offset == TILE_COLS - 1 - lax.rem(query_at, TILE_COLS)).astype(jnp.float32)
        row_hot = (offset == TILE_ROWS - 1 - lax.div(query_at, TILE_COLS)).astype(jnp.float32)
        column_bias = jnp.dot(
            shifted[0:TILE_COLS, :], column_hot, precision=HIGHEST,
            preferred_element_type=jnp.float32,
        )
        row_bias = jnp.dot(
            shifted[TILE_COLS : TILE_COLS + TILE_ROWS, :], row_hot, precision=HIGHEST,
            preferred_element_type=jnp.float32,
        )
        for j in range(TILE_ROWS):
            band = column_bias + row_bias[j : j + 1, :]
            fine[j * TILE_COLS : (j + 1) * TILE_COLS, 0:TILE] = band
            fine[j * TILE_COLS : (j + 1) * TILE_COLS, TILE : 2 * TILE] = band
        fine_sum[...] = jnp.zeros_like(fine_sum)
        coarse_sum[...] = jnp.zeros_like(coarse_sum)

        def one_query_tile(q, carry):
            query = qd_in[c, 0, q]
            grad = qd_in[c, 1, q]
            key = key_set[q]
            value = value_set[q]
            hot = entries[q, 0]
            entry_bias = jnp.sum(hot * head_row, axis=1, keepdims=True) + entries[q, 1][:, 0:1]
            both = (((1,), (1,)), ((), ()))
            raw = lax.dot_general(key, query, both, preferred_element_type=jnp.float32)
            product = lax.dot_general(value, grad, both, preferred_element_type=jnp.float32)
            fine_bias = fine[...]
            scores = [
                raw[e * TILE : (e + 1) * TILE, :] * SCALE + (fine_bias + entry_bias[e : e + 1, :])
                for e in range(ENTRIES)
            ]
            attend_grad = [product[e * TILE : (e + 1) * TILE, :] for e in range(ENTRIES)]
            top = scores[0]
            for e in range(1, ENTRIES):
                top = jnp.maximum(top, scores[e])
            top = jnp.max(top, axis=0, keepdims=True)
            expo = [jnp.exp(block - top) for block in scores]
            total, weighted = expo[0], expo[0] * attend_grad[0]
            for e in range(1, ENTRIES):
                total = total + expo[e]
                weighted = weighted + expo[e] * attend_grad[e]
            inverse = 1.0 / jnp.sum(total, axis=0, keepdims=True)
            delta = jnp.sum(weighted, axis=0, keepdims=True) * inverse
            attend = [block * inverse for block in expo]
            score_grad = [attend[e] * (attend_grad[e] - delta) for e in range(ENTRIES)]
            attend_low = jnp.concatenate([b.astype(jnp.bfloat16) for b in attend], axis=0)
            grad_low = jnp.concatenate([b.astype(jnp.bfloat16) for b in score_grad], axis=0)
            value_part[q] = jnp.dot(attend_low, grad, preferred_element_type=jnp.float32)
            key_part[q] = jnp.dot(grad_low, query, preferred_element_type=jnp.float32) * SCALE
            query_grad = lax.dot_general(
                key, grad_low, (((0,), (0,)), ((), ())), preferred_element_type=jnp.float32
            )
            ret[c, 0, q] = (query_grad.T * SCALE).astype(jnp.bfloat16)
            total_grad = score_grad[0]
            for e in range(1, ENTRIES):
                total_grad = total_grad + score_grad[e]
            fine_sum[...] += total_grad[:, 0:TILE] + total_grad[:, TILE : 2 * TILE]
            coarse = jnp.zeros((1, TABLE), jnp.float32)
            for e in range(ENTRIES):
                block_sum = jnp.sum(score_grad[e], axis=0, keepdims=True)
                coarse = coarse + jnp.sum(block_sum, axis=1, keepdims=True) * hot[e : e + 1, :]
            coarse_sum[0:1, :] += coarse
            return carry

        lax.fori_loop(0, SIDE, one_query_tile, 0)
        for j in ORDER:
            give_back(0, c, j)
        parts = (key_part, value_part)

        def part_of(a, q, s):
            at = (TILES_DEV + s) * TILE
            return parts[a][q, at : at + TILE, :].astype(jnp.bfloat16)

        for a in range(2):
            for q, s, tile, n in NEAR:
                back[c, tile, a, n] = part_of(a, q, s)
            for q in range(SIDE):
                back[c, q, a, 0] = part_of(a, q, SLOTS - 1)
        for j in ORDER:
            tile = lax.rem(x + j, SIDE)
            for a in range(2):
                back_copy(c, tile, a, 1).start()

                @pl.when(outer(tile))
                def _(a=a, tile=tile):
                    back_copy(c, tile, a, 2).start()

                back_copy(c, tile, a, 0).start()
        slot = lax.rem(c, 2)
        for a in range(2):
            for q in range(SIDE):
                acc[slot, a, q] = parts[a][q, 0 : 2 * TILE, :]
            for q, s, tile in LOCAL:
                at = (TILES_DEV + s) * TILE
                deposit(slot, a, tile, upper(y, q, s), parts[a][q, at : at + TILE, :])

        folded = fine_sum[...].reshape(TILE_ROWS, TILE_COLS, TILE)
        across = (((1,), (1,)), ((), ()))
        column_grad = lax.dot_general(
            jnp.sum(folded, axis=0), column_hot, across, precision=HIGHEST,
            preferred_element_type=jnp.float32,
        )
        row_grad = lax.dot_general(
            jnp.sum(folded, axis=1), row_hot, across, precision=HIGHEST,
            preferred_element_type=jnp.float32,
        )
        table_row = coarse_sum[0:1, :]
        for j in range(TILE_COLS):
            table_row = table_row + pltpu.roll(column_grad[j : j + 1, :], BUCKETS + j, 1)
        for j in range(TILE_ROWS):
            table_row = table_row + pltpu.roll(
                row_grad[j : j + 1, :], BUCKETS + COLUMN_WIDTH + j, 1
            )
        grads[pl.ds(c, 1), :] = table_row

    def deposit(slot, a, tile, pick, partial):
        acc[slot, a, tile, 0:TILE, :] += jnp.where(pick, 0.0, partial)
        acc[slot, a, tile, TILE : 2 * TILE, :] += jnp.where(pick, partial, 0.0)

    def finish(c):
        slot = lax.rem(c, 2)
        for j in ORDER:
            tile = lax.rem(x + j, SIDE)

            @pl.when(outer(tile))
            def _(tile=tile):
                arrived(home.at[c, tile], home_recv.at[c, tile])
                for a in range(2):
                    deposit(
                        slot, a, tile, near_pick(tile, 2),
                        home[c, tile, a, 2].astype(jnp.float32),
                    )

            @pl.when(jnp.logical_not(outer(tile)))
            def _(tile=tile):
                arrived(home.at[c, tile, :, 0:2], home_recv.at[c, tile])

            picks = (upper(y + SIDE // 2, tile, SLOTS - 1), near_pick(tile, 1))
            for a in range(2):
                for n, pick in enumerate(picks):
                    deposit(slot, a, tile, pick, home[c, tile, a, n].astype(jnp.float32))
                ret[c, 1 + a, tile] = acc[slot, a, tile].astype(jnp.bfloat16)
                give_back(1 + a, c, j)

    def dp_copy(j):
        return remote(
            grads, grads_dp.at[part], dp_send, dp_recv,
            {"dp": lax.rem(part + j, DP)},
        )

    def seq_copy(j):
        return remote(
            grads_seq.at[place], grads_seq.at[place], seq_send, seq_recv,
            {"seq": lax.rem(place + j, SEQ)},
        )

    def step(t, carry):
        @pl.when(t < CHUNKS)
        def _():
            send_tiles(t)

        @pl.when(t == 1)
        def _():
            table_arrived(1)
            table_copy(2).start()
            arrived(entries.at[peers], entry_recv)

        @pl.when(t == 2)
        def _():
            table_arrived(2)

        @pl.when(t >= 2)
        def _():
            compute(t - 2)

        @pl.when(t == CHUNKS + 1)
        def _():
            for j in range(1, DP):
                dp_copy(j).start()

        @pl.when(t >= 3)
        def _():
            finish(t - 3)

        return carry

    lax.fori_loop(0, CHUNKS + 2, step, 0)

    total = grads[...]
    arrived(grads_dp.at[0 : DP - 1], dp_recv)
    for j in range(1, DP):
        total = total + grads_dp[lax.rem(part + j, DP)]
    grads_seq[place] = total
    for j in range(1, SEQ):
        seq_copy(j).start()
    finish(CHUNKS - 1)
    arrived(grads_seq.at[0 : SEQ - 1], seq_recv)
    owner = lax.div(part, 2)
    mine = grads_seq[owner]
    for j in range(1, SIDE):
        mine = mine + grads_seq[owner + j * SIDE]
    own = HEADS // DP
    table_out[...] = jnp.where(lax.rem(part, 2) == 0, mine[0:own, :], mine[own : 2 * own, :])

    arrived(kv_in.at[:, :, peers], kv_send)
    arrived(qd_in.at[:, :, peers], qd_send)
    for g in range(3):
        arrived(gives[g], give_send.at[g])
    arrived(got, back_send)
    for a in range(3):
        arrived(ret.at[:, a, peers], ret_send.at[a])
    for n in range(len(STRIDES)):
        table_copy(n).wait_send()
    arrived(grads_dp.at[0 : DP - 1], dp_send)
    arrived(entries.at[peers], entry_send)
    arrived(grads_seq.at[0 : SEQ - 1], seq_send)
    for a in range(3):
        arrived(outs[a].at[0 : TOK_DEV - TOK_DEV // SIDE], out_recv.at[a])


def per_device(queries, keys, values, grad_out, bias_table, slot_tiles, live, buckets):
    hbm = pl.BlockSpec(memory_space=pltpu.HBM)
    vmem = pl.BlockSpec(memory_space=pltpu.VMEM)
    low, full = jnp.bfloat16, jnp.float32
    dma = pltpu.SemaphoreType.DMA
    moved = [pltpu.VMEM((CHUNKS, 2, len(group), TILE, HEAD_DIM), low) for group, _ in GROUPS]
    set_rows = ENTRIES * TILE
    out = pltpu.VMEM((TOK_DEV, WIDTH), low)
    operands = (
        queries[0], keys[0], values[0], grad_out[0], bias_table, slot_tiles.T, live, buckets,
    )
    result = pl.pallas_call(
        kernel,
        out_shape=(out, out, out, jax.ShapeDtypeStruct((HEADS // DP, TABLE), full)),
        in_specs=[hbm] * len(operands),
        out_specs=(vmem, vmem, vmem, vmem),
        scratch_shapes=[
            pltpu.VMEM((CHUNKS, 2, SIDE, TOK_DEV, HEAD_DIM), low),
            pltpu.VMEM((CHUNKS, 2, SIDE, TOK_DEV, HEAD_DIM), low),
            *moved,
            pltpu.VMEM((CHUNKS, 2, FIRST[-1], TILE, HEAD_DIM), low),
            pltpu.VMEM((CHUNKS, SIDE, 2, 3, TILE, HEAD_DIM), low),
            pltpu.VMEM((CHUNKS, SIDE, 2, 3, TILE, HEAD_DIM), low),
            pltpu.VMEM((CHUNKS, 3, SIDE, TOK_DEV, HEAD_DIM), low),
            pltpu.VMEM((2, 2, SIDE, TOK_DEV, HEAD_DIM), full),
            pltpu.VMEM((SIDE, set_rows, HEAD_DIM), low),
            pltpu.VMEM((SIDE, set_rows, HEAD_DIM), low),
            pltpu.VMEM((SIDE, set_rows, HEAD_DIM), full),
            pltpu.VMEM((SIDE, set_rows, HEAD_DIM), full),
            pltpu.VMEM(bias_table.shape, full),
            pltpu.SMEM((SLOTS, SEQ), jnp.int32),
            pltpu.SMEM(live.shape, jnp.int32),
            pltpu.SMEM(buckets.shape, jnp.int32),
            pltpu.VMEM((2, CHUNKS, TOK_DEV, HEAD_DIM), low),
            pltpu.VMEM((2, CHUNKS, TILE, HEAD_DIM), low),
            pltpu.VMEM((DP, 8, TABLE), full),
            pltpu.VMEM((SIDE, 2, 8, TABLE), full),
            pltpu.VMEM((TILE_COLS + TILE_ROWS, TABLE), full),
            pltpu.VMEM((TILE, 2 * TILE), full),
            pltpu.VMEM((TILE, TILE), full),
            pltpu.VMEM((8, TABLE), full),
            pltpu.VMEM((8, TABLE), full),
            pltpu.VMEM((DP, 8, TABLE), full),
            pltpu.VMEM((SEQ, 8, TABLE), full),
            dma((4,)), dma(()),
            dma(()), dma((CHUNKS, 2)),
            dma(()), dma((CHUNKS,)),
            dma((3,)), dma((CHUNKS,)),
            dma(()), dma((CHUNKS, SIDE)),
            dma((3,)), dma((3,)),
            dma((len(STRIDES),)), dma((len(STRIDES),)),
            dma(()), dma(()),
            dma(()), dma(()),
            dma(()), dma(()),
        ],
        compiler_params=pltpu.CompilerParams(
            collective_id=0, has_side_effects=True, vmem_limit_bytes=48 * 2**20
        ),
        cost_estimate=pl.CostEstimate(
            flops=7_046_430_720, bytes_accessed=11_000_000, transcendentals=5_505_024
        ),
    )(*[pltpu.with_memory_space_constraint(operand, pltpu.HBM) for operand in operands])
    query_grad, key_grad, value_grad, table_grad = result
    return (query_grad[None], key_grad[None], value_grad[None], table_grad)


def solution(mesh):
    rows = P("dp", "seq", None)
    return jax.shard_map(
        per_device,
        mesh=mesh,
        in_specs=(rows, rows, rows, rows, P("dp", None), P(), P("seq", None), P("seq", None)),
        out_specs=(rows, rows, rows, P("dp", None)),
        check_vma=False,
    )
```

```python
import jax
import jax.numpy as jnp
from jax import lax
from jax.experimental import pallas as pl
from jax.experimental.pallas import tpu as pltpu
from jax.sharding import PartitionSpec as P

HEADS = 24
HEAD_DIM = 128
TOK_DEV = 256
TILE = 128
TILE_COLS = 16
TILE_ROWS = TILE // TILE_COLS
SLOTS = 5
BUCKETS = 82
WIDTH = 3072
TILES_DEV = 2
ENTRIES = TILES_DEV + SLOTS
COLUMN_WIDTH = 2 * TILE_COLS - 1
TABLE = 128

SIDE = 4
SEQ = SIDE * SIDE
DP = 8
STRIDES = (1, 2, 4)
CHUNKS = HEADS // SIDE
NEGATIVE = -1e30
SCALE = HEAD_DIM ** (-0.5)
NEAR_OFFSETS = (-1, 1, -2, 2)
HIGHEST = lax.Precision.HIGHEST
MESH = pl.DeviceIdType.MESH

ORDER = (2, 1, 3, 0)

FROM_BELOW = tuple((q, s, q + o + SIDE) for q in range(SIDE) for s, o in enumerate(NEAR_OFFSETS) if q + o < 0)
FROM_ABOVE = tuple((q, s, q + o - SIDE) for q in range(SIDE) for s, o in enumerate(NEAR_OFFSETS) if q + o >= SIDE)
FROM_HALF = tuple((q, SLOTS - 1, q) for q in range(SIDE))
FIRST = (0, 3, 6, 10)
GROUPS = ((FROM_BELOW, 1), (FROM_ABOVE, SIDE - 1), (FROM_HALF, SIDE // 2))
NEAR = tuple(
    (q, s, tile, 1 + sum(tile == other[2] for other in group[:n]))
    for group in (FROM_BELOW, FROM_ABOVE[::-1])
    for n, (q, s, tile) in enumerate(group)
)
LOCAL = tuple(
    (q, s, q + o) for q in range(SIDE) for s, o in enumerate(NEAR_OFFSETS) if 0 <= q + o < SIDE
)


def iota(shape, axis):
    return lax.broadcasted_iota(jnp.int32, shape, axis)


def kernel(
    queries, keys, values, upstream, table_hbm, slots_hbm, live_hbm, buckets_hbm,
    query_out, key_out, value_out, table_out,
    kv_in, qd_in, give0, give1, give2, got, back, home,
    ret, acc, key_set, value_set, key_part, value_part,
    table, slots, live, buckets, own_heads, own_far,
    tables, entries, shifted, fine, fine_sum, coarse_sum, grads, grads_dp, grads_seq,
    small_recv, own_recv,
    kv_send, kv_recv, qd_send, qd_recv, give_send, got_recv, back_send, home_recv, ret_send, out_recv,
    table_send, table_recv, entry_send, entry_recv, dp_send, dp_recv, seq_send, seq_recv,
):
    gives = (give0, give1, give2)
    outs = (query_out, key_out, value_out)
    place = lax.axis_index("seq")
    part = lax.axis_index("dp")
    x, y = lax.rem(place, SIDE), lax.div(place, SIDE)

    def seq_at(column, row):
        return {"seq": lax.rem(row, SIDE) * SIDE + lax.rem(column, SIDE)}

    def remote(source, target, send, recv, device):
        return pltpu.make_async_remote_copy(
            src_ref=source, dst_ref=target, send_sem=send, recv_sem=recv,
            device_id=device, device_id_type=MESH,
        )

    def arrived(buffer, semaphore):
        pltpu.make_async_copy(buffer, buffer, semaphore).wait()

    peers = slice(0, SIDE - 1)

    def head_columns(head):
        return pl.ds(pl.multiple_of(head * HEAD_DIM, HEAD_DIM), HEAD_DIM)

    barrier = pltpu.get_barrier_semaphore()
    pairs = tuple(part + o - 2 * o * lax.rem(lax.div(part, o), 2) for o in STRIDES)
    greeted = [seq_at(x + j, y) for j in range(1, SIDE)]
    greeted += [seq_at(x, y + j) for j in range(1, SIDE)]
    greeted += [{"dp": pair} for pair in pairs]
    for device in greeted:
        pl.semaphore_signal(barrier, inc=1, device_id=device, device_id_type=MESH)
    small = [
        pltpu.make_async_copy(source, target, small_recv.at[n])
        for n, (source, target) in enumerate(
            ((slots_hbm, slots), (live_hbm, live), (buckets_hbm, buckets), (table_hbm, table))
        )
    ]
    for copy in small:
        copy.start()
    for a, ref in enumerate((keys, values)):
        for c in range(CHUNKS):
            pltpu.make_async_copy(
                ref.at[:, head_columns(x * CHUNKS + c)], own_heads.at[a, c], own_recv
            ).start()
    for copy in small:
        copy.wait()

    def upper(query_row, q, s):
        return lax.rem(slots[s, lax.rem(query_row, SIDE) * SIDE + q], TILES_DEV) == 1

    lane = iota((8, TABLE), 1)
    row = iota((8, TABLE), 0)
    tables[part] = jnp.zeros((8, TABLE), jnp.float32)
    tables[part, 0 : HEADS // DP, :] = table[...]
    bucket = jnp.full((8, TABLE), -1, jnp.int32)
    alive = jnp.zeros((8, TABLE), jnp.int32)
    for e in range(ENTRIES):
        bucket = jnp.where(row == e, buckets[0, e], bucket)
        alive = jnp.where(row == e, live[0, e], alive)
    entries[x, 0] = (lane == bucket).astype(jnp.float32)
    entries[x, 1] = jnp.where(alive > 0, 0.0, NEGATIVE)
    grads[...] = jnp.zeros_like(grads)
    arrived(own_heads, own_recv)
    half_pick = upper(y + SIDE // 2, x, SLOTS - 1)
    for a in range(2):
        for c in range(CHUNKS):
            own_far[a, c] = jnp.where(
                half_pick, own_heads[a, c, TILE : 2 * TILE, :], own_heads[a, c, 0:TILE, :]
            )

    pl.semaphore_wait(barrier, len(greeted))

    def table_block(device, n):
        stride = STRIDES[n]
        return tables.at[pl.ds(lax.div(device, stride) * stride, stride)]

    def table_copy(n):
        block = table_block(part, n)
        return remote(block, block, table_send.at[n], table_recv.at[n], {"dp": pairs[n]})

    def table_arrived(n):
        arrived(table_block(pairs[n], n), table_recv.at[n])

    def entry_copy(j):
        return remote(
            entries.at[x], entries.at[x], entry_send, entry_recv, seq_at(x + j, y)
        )

    def fetch(refs, buffer, send, recvs, c):
        for a, ref in enumerate(refs):
            recv = recvs(c, a)
            for j in ORDER[:-1]:
                to = lax.rem(x + j, SIDE)
                remote(
                    ref.at[:, head_columns(to * CHUNKS + c)], buffer.at[c, a, x],
                    send, recv, seq_at(to, y),
                ).start()
            pltpu.make_async_copy(
                ref.at[:, head_columns(x * CHUNKS + c)], buffer.at[c, a, x], recv
            ).start()

    kv = ((keys, values), kv_in, kv_send, lambda c, a: kv_recv.at[c, a])
    qd = ((queries, upstream), qd_in, qd_send, lambda c, a: qd_recv.at[c])

    def give_copy(g, c, a):
        return remote(
            gives[g].at[c, a], got.at[c, a, FIRST[g] : FIRST[g + 1]], give_send.at[g],
            got_recv.at[c],
            seq_at(x, y + GROUPS[g][1]),
        )

    def back_copy(c, tile, a, n):
        row = SIDE // 2 if n == 0 else jnp.where(tile < 2, 1, SIDE - 1)
        return remote(
            back.at[c, tile, a, n], home.at[c, tile, a, n], back_send, home_recv.at[c, tile],
            seq_at(x, y + row),
        )

    def outer(tile):
        return (tile == 0) | (tile == SIDE - 1)

    def near_pick(tile, n):
        listing_row = y + jnp.where(tile < 2, SIDE - 1, 1)
        if n == 1:
            q = jnp.where(tile < 2, SIDE - 1, 0)
            s = jnp.where(tile == 0, 1, jnp.where(tile == 1, 3, jnp.where(tile == 2, 2, 0)))
        else:
            q = jnp.where(tile == 0, 2, 1)
            s = jnp.where(tile == 0, 3, 2)
        return upper(listing_row, q, s)

    def give_back(a, c, j):
        columns = head_columns(x * CHUNKS + c)
        source = ret.at[c, a, lax.rem(x + j, SIDE)]
        if j == 0:
            outs[a][:, columns] = ret[c, a, x]
        else:
            remote(
                source, outs[a].at[:, columns], ret_send.at[a], out_recv.at[a], seq_at(x + j, y)
            ).start()

    for c in range(CHUNKS):
        for a in range(2):
            remote(
                own_far.at[a, c], got.at[c, a, FIRST[2] + x], give_send.at[2], got_recv.at[c],
                seq_at(x, y + SIDE // 2),
            ).start()
        if c == 0:
            fetch(*kv, 0)
    table_copy(0).start()
    for j in range(1, SIDE):
        entry_copy(j).start()
    fetch(*kv, 1)
    fetch(*kv, 2)
    fetch(*qd, 0)
    table_arrived(0)
    table_copy(1).start()

    def halves(c, a, tile):
        return kv_in[c, a, tile, 0:TILE, :], kv_in[c, a, tile, TILE : 2 * TILE, :]

    def send_tiles(c):
        for a in range(2):
            arrived(kv_in.at[c, a], kv_recv.at[c, a])
            for g, (group, distance) in enumerate(GROUPS[:2]):
                for n, (q, s, tile) in enumerate(group):
                    low, high = halves(c, a, tile)
                    gives[g][c, a, n] = jnp.where(upper(y + distance, q, s), high, low)
                give_copy(g, c, a).start()

            for j in ORDER[:-1]:
                tile = lax.rem(x + j, SIDE)
                low, high = halves(c, a, tile)
                pick = upper(y + SIDE // 2, tile, SLOTS - 1)
                gives[2][c, a, tile] = jnp.where(pick, high, low)
                remote(
                    gives[2].at[c, a, tile], got.at[c, a, FIRST[2] + tile], give_send.at[2],
                    got_recv.at[c], seq_at(x, y + SIDE // 2),
                ).start()

        @pl.when(c + 3 < CHUNKS)
        def _():
            fetch(*kv, c + 3)

        @pl.when(c + 1 < CHUNKS)
        def _():
            fetch(*qd, c + 1)

    def compute(c):
        arrived(qd_in.at[c], qd_recv.at[c])
        arrived(got.at[c], got_recv.at[c])
        sets = (key_set, value_set)
        for a in range(2):
            for q in range(SIDE):
                sets[a][q, 0 : 2 * TILE, :] = kv_in[c, a, q]
            for q, s, tile in LOCAL:
                low, high = halves(c, a, tile)
                at = (TILES_DEV + s) * TILE
                sets[a][q, at : at + TILE, :] = jnp.where(upper(y, q, s), high, low)
            for g, (group, _) in enumerate(GROUPS):
                for n, (q, s, _) in enumerate(group):
                    at = (TILES_DEV + s) * TILE
                    sets[a][q, at : at + TILE, :] = got[c, a, FIRST[g] + n]

        head_row = tables[2 * x + lax.div(c, 3), pl.ds(lax.rem(c, 3), 1), :]
        for j in range(TILE_COLS):
            shifted[j : j + 1, :] = pltpu.roll(head_row, (2 * TABLE - BUCKETS - j) % TABLE, 1)
        for j in range(TILE_ROWS):
            shifted[TILE_COLS + j : TILE_COLS + j + 1, :] = pltpu.roll(
                head_row, (2 * TABLE - BUCKETS - COLUMN_WIDTH - j) % TABLE, 1
            )
        offset = iota((TABLE, TILE), 0)
        query_at = iota((TABLE, TILE), 1)
        column_hot = (offset == TILE_COLS - 1 - lax.rem(query_at, TILE_COLS)).astype(jnp.float32)
        row_hot = (offset == TILE_ROWS - 1 - lax.div(query_at, TILE_COLS)).astype(jnp.float32)
        column_bias = jnp.dot(
            shifted[0:TILE_COLS, :], column_hot, precision=HIGHEST,
            preferred_element_type=jnp.float32,
        )
        row_bias = jnp.dot(
            shifted[TILE_COLS : TILE_COLS + TILE_ROWS, :], row_hot, precision=HIGHEST,
            preferred_element_type=jnp.float32,
        )
        for j in range(TILE_ROWS):
            band = column_bias + row_bias[j : j + 1, :]
            fine[j * TILE_COLS : (j + 1) * TILE_COLS, 0:TILE] = band
            fine[j * TILE_COLS : (j + 1) * TILE_COLS, TILE : 2 * TILE] = band
        fine_sum[...] = jnp.zeros_like(fine_sum)
        coarse_sum[...] = jnp.zeros_like(coarse_sum)

        def one_query_tile(q, carry):
            query = qd_in[c, 0, q]
            grad = qd_in[c, 1, q]
            key = key_set[q]
            value = value_set[q]
            hot = entries[q, 0]
            entry_bias = jnp.sum(hot * head_row, axis=1, keepdims=True) + entries[q, 1][:, 0:1]
            both = (((1,), (1,)), ((), ()))
            raw = lax.dot_general(key, query, both, preferred_element_type=jnp.float32)
            product = lax.dot_general(value, grad, both, preferred_element_type=jnp.float32)
            fine_bias = fine[...]
            scores = [
                raw[e * TILE : (e + 1) * TILE, :] * SCALE + (fine_bias + entry_bias[e : e + 1, :])
                for e in range(ENTRIES)
            ]
            attend_grad = [product[e * TILE : (e + 1) * TILE, :] for e in range(ENTRIES)]
            top = scores[0]
            for e in range(1, ENTRIES):
                top = jnp.maximum(top, scores[e])
            top = jnp.max(top, axis=0, keepdims=True)
            expo = [jnp.exp(block - top) for block in scores]
            total, weighted = expo[0], expo[0] * attend_grad[0]
            for e in range(1, ENTRIES):
                total = total + expo[e]
                weighted = weighted + expo[e] * attend_grad[e]
            inverse = 1.0 / jnp.sum(total, axis=0, keepdims=True)
            delta = jnp.sum(weighted, axis=0, keepdims=True) * inverse
            attend = [block * inverse for block in expo]
            score_grad = [attend[e] * (attend_grad[e] - delta) for e in range(ENTRIES)]
            attend_low = jnp.concatenate([b.astype(jnp.bfloat16) for b in attend], axis=0)
            grad_low = jnp.concatenate([b.astype(jnp.bfloat16) for b in score_grad], axis=0)
            value_part[q] = jnp.dot(attend_low, grad, preferred_element_type=jnp.float32)
            key_part[q] = jnp.dot(grad_low, query, preferred_element_type=jnp.float32) * SCALE
            query_grad = lax.dot_general(
                key, grad_low, (((0,), (0,)), ((), ())), preferred_element_type=jnp.float32
            )
            ret[c, 0, q] = (query_grad.T * SCALE).astype(jnp.bfloat16)
            total_grad = score_grad[0]
            for e in range(1, ENTRIES):
                total_grad = total_grad + score_grad[e]
            fine_sum[...] += total_grad[:, 0:TILE] + total_grad[:, TILE : 2 * TILE]
            coarse = jnp.zeros((1, TABLE), jnp.float32)
            for e in range(ENTRIES):
                block_sum = jnp.sum(score_grad[e], axis=0, keepdims=True)
                coarse = coarse + jnp.sum(block_sum, axis=1, keepdims=True) * hot[e : e + 1, :]
            coarse_sum[0:1, :] += coarse
            return carry

        lax.fori_loop(0, SIDE, one_query_tile, 0)
        for j in ORDER:
            give_back(0, c, j)
        parts = (key_part, value_part)

        def part_of(a, q, s):
            at = (TILES_DEV + s) * TILE
            return parts[a][q, at : at + TILE, :].astype(jnp.bfloat16)

        for a in range(2):
            for q, s, tile, n in NEAR:
                back[c, tile, a, n] = part_of(a, q, s)
            for q in range(SIDE):
                back[c, q, a, 0] = part_of(a, q, SLOTS - 1)
        for j in ORDER:
            tile = lax.rem(x + j, SIDE)
            for a in range(2):
                lists = jnp.where(tile < 2, y != SIDE - 1, y != 0)

                @pl.when(lists)
                def _(a=a, tile=tile):
                    back_copy(c, tile, a, 1).start()

                @pl.when(lists & outer(tile))
                def _(a=a, tile=tile):
                    back_copy(c, tile, a, 2).start()

                back_copy(c, tile, a, 0).start()
        slot = lax.rem(c, 2)
        for a in range(2):
            for q in range(SIDE):
                acc[slot, a, q] = parts[a][q, 0 : 2 * TILE, :]
            for q, s, tile in LOCAL:
                at = (TILES_DEV + s) * TILE
                deposit(slot, a, tile, upper(y, q, s), parts[a][q, at : at + TILE, :])

        folded = fine_sum[...].reshape(TILE_ROWS, TILE_COLS, TILE)
        across = (((1,), (1,)), ((), ()))
        column_grad = lax.dot_general(
            jnp.sum(folded, axis=0), column_hot, across, precision=HIGHEST,
            preferred_element_type=jnp.float32,
        )
        row_grad = lax.dot_general(
            jnp.sum(folded, axis=1), row_hot, across, precision=HIGHEST,
            preferred_element_type=jnp.float32,
        )
        table_row = coarse_sum[0:1, :]
        for j in range(TILE_COLS):
            table_row = table_row + pltpu.roll(column_grad[j : j + 1, :], BUCKETS + j, 1)
        for j in range(TILE_ROWS):
            table_row = table_row + pltpu.roll(
                row_grad[j : j + 1, :], BUCKETS + COLUMN_WIDTH + j, 1
            )
        grads[pl.ds(c, 1), :] = table_row

    def deposit(slot, a, tile, pick, partial):
        acc[slot, a, tile, 0:TILE, :] += jnp.where(pick, 0.0, partial)
        acc[slot, a, tile, TILE : 2 * TILE, :] += jnp.where(pick, partial, 0.0)

    def finish(c):
        slot = lax.rem(c, 2)
        for j in ORDER:
            tile = lax.rem(x + j, SIDE)

            listed = jnp.where(tile < 2, y != 0, y != SIDE - 1)

            def near(n, tile=tile):
                pick = near_pick(tile, n)
                for a in range(2):
                    deposit(slot, a, tile, pick, home[c, tile, a, n].astype(jnp.float32))

            @pl.when(listed & outer(tile))
            def _(tile=tile, near=near):
                arrived(home.at[c, tile], home_recv.at[c, tile])
                near(1)
                near(2)

            @pl.when(listed & jnp.logical_not(outer(tile)))
            def _(tile=tile, near=near):
                arrived(home.at[c, tile, :, 0:2], home_recv.at[c, tile])
                near(1)

            @pl.when(jnp.logical_not(listed))
            def _(tile=tile):
                arrived(home.at[c, tile, :, 0:1], home_recv.at[c, tile])

            far_pick = upper(y + SIDE // 2, tile, SLOTS - 1)
            for a in range(2):
                deposit(slot, a, tile, far_pick, home[c, tile, a, 0].astype(jnp.float32))
                ret[c, 1 + a, tile] = acc[slot, a, tile].astype(jnp.bfloat16)
                give_back(1 + a, c, j)

    def dp_copy(j):
        return remote(
            grads, grads_dp.at[part], dp_send, dp_recv,
            {"dp": lax.rem(part + j, DP)},
        )

    def seq_copy(j):
        return remote(
            grads_seq.at[place], grads_seq.at[place], seq_send, seq_recv,
            {"seq": lax.rem(place + j, SEQ)},
        )

    def step(t, carry):
        @pl.when(t < CHUNKS)
        def _():
            send_tiles(t)

        @pl.when(t == 1)
        def _():
            table_arrived(1)
            table_copy(2).start()
            arrived(entries.at[peers], entry_recv)

        @pl.when(t == 2)
        def _():
            table_arrived(2)

        @pl.when(t >= 2)
        def _():
            compute(t - 2)

        @pl.when(t == CHUNKS + 1)
        def _():
            for j in range(1, DP):
                dp_copy(j).start()

        @pl.when(t >= 3)
        def _():
            finish(t - 3)

        return carry

    lax.fori_loop(0, CHUNKS + 2, step, 0)

    total = grads[...]
    arrived(grads_dp.at[0 : DP - 1], dp_recv)
    for j in range(1, DP):
        total = total + grads_dp[lax.rem(part + j, DP)]
    grads_seq[place] = total
    for j in range(1, SEQ):
        seq_copy(j).start()
    finish(CHUNKS - 1)
    arrived(grads_seq.at[0 : SEQ - 1], seq_recv)
    owner = lax.div(part, 2)
    mine = grads_seq[owner]
    for j in range(1, SIDE):
        mine = mine + grads_seq[owner + j * SIDE]
    own = HEADS // DP
    table_out[...] = jnp.where(lax.rem(part, 2) == 0, mine[0:own, :], mine[own : 2 * own, :])

    arrived(kv_in.at[:, :, peers], kv_send)
    arrived(qd_in.at[:, :, peers], qd_send)
    for g in range(3):
        arrived(gives[g], give_send.at[g])
    ends = (y == 0) | (y == SIDE - 1)

    @pl.when(ends)
    def _():
        arrived(got.at[:, :, FIRST[1] :], back_send)

    @pl.when(jnp.logical_not(ends))
    def _():
        arrived(got, back_send)

    for a in range(3):
        arrived(ret.at[:, a, peers], ret_send.at[a])
    for n in range(len(STRIDES)):
        table_copy(n).wait_send()
    arrived(grads_dp.at[0 : DP - 1], dp_send)
    arrived(entries.at[peers], entry_send)
    arrived(grads_seq.at[0 : SEQ - 1], seq_send)
    for a in range(3):
        arrived(outs[a].at[0 : TOK_DEV - TOK_DEV // SIDE], out_recv.at[a])


def per_device(queries, keys, values, grad_out, bias_table, slot_tiles, live, buckets):
    hbm = pl.BlockSpec(memory_space=pltpu.HBM)
    vmem = pl.BlockSpec(memory_space=pltpu.VMEM)
    low, full = jnp.bfloat16, jnp.float32
    dma = pltpu.SemaphoreType.DMA
    moved = [pltpu.VMEM((CHUNKS, 2, len(group), TILE, HEAD_DIM), low) for group, _ in GROUPS]
    set_rows = ENTRIES * TILE
    out = pltpu.VMEM((TOK_DEV, WIDTH), low)
    operands = (
        queries[0], keys[0], values[0], grad_out[0], bias_table, slot_tiles.T, live, buckets,
    )
    result = pl.pallas_call(
        kernel,
        out_shape=(out, out, out, jax.ShapeDtypeStruct((HEADS // DP, TABLE), full)),
        in_specs=[hbm] * len(operands),
        out_specs=(vmem, vmem, vmem, vmem),
        scratch_shapes=[
            pltpu.VMEM((CHUNKS, 2, SIDE, TOK_DEV, HEAD_DIM), low),
            pltpu.VMEM((CHUNKS, 2, SIDE, TOK_DEV, HEAD_DIM), low),
            *moved,
            pltpu.VMEM((CHUNKS, 2, FIRST[-1], TILE, HEAD_DIM), low),
            pltpu.VMEM((CHUNKS, SIDE, 2, 3, TILE, HEAD_DIM), low),
            pltpu.VMEM((CHUNKS, SIDE, 2, 3, TILE, HEAD_DIM), low),
            pltpu.VMEM((CHUNKS, 3, SIDE, TOK_DEV, HEAD_DIM), low),
            pltpu.VMEM((2, 2, SIDE, TOK_DEV, HEAD_DIM), full),
            pltpu.VMEM((SIDE, set_rows, HEAD_DIM), low),
            pltpu.VMEM((SIDE, set_rows, HEAD_DIM), low),
            pltpu.VMEM((SIDE, set_rows, HEAD_DIM), full),
            pltpu.VMEM((SIDE, set_rows, HEAD_DIM), full),
            pltpu.VMEM(bias_table.shape, full),
            pltpu.SMEM((SLOTS, SEQ), jnp.int32),
            pltpu.SMEM(live.shape, jnp.int32),
            pltpu.SMEM(buckets.shape, jnp.int32),
            pltpu.VMEM((2, CHUNKS, TOK_DEV, HEAD_DIM), low),
            pltpu.VMEM((2, CHUNKS, TILE, HEAD_DIM), low),
            pltpu.VMEM((DP, 8, TABLE), full),
            pltpu.VMEM((SIDE, 2, 8, TABLE), full),
            pltpu.VMEM((TILE_COLS + TILE_ROWS, TABLE), full),
            pltpu.VMEM((TILE, 2 * TILE), full),
            pltpu.VMEM((TILE, TILE), full),
            pltpu.VMEM((8, TABLE), full),
            pltpu.VMEM((8, TABLE), full),
            pltpu.VMEM((DP, 8, TABLE), full),
            pltpu.VMEM((SEQ, 8, TABLE), full),
            dma((4,)), dma(()),
            dma(()), dma((CHUNKS, 2)),
            dma(()), dma((CHUNKS,)),
            dma((3,)), dma((CHUNKS,)),
            dma(()), dma((CHUNKS, SIDE)),
            dma((3,)), dma((3,)),
            dma((len(STRIDES),)), dma((len(STRIDES),)),
            dma(()), dma(()),
            dma(()), dma(()),
            dma(()), dma(()),
        ],
        compiler_params=pltpu.CompilerParams(
            collective_id=0, has_side_effects=True, vmem_limit_bytes=48 * 2**20
        ),
        cost_estimate=pl.CostEstimate(
            flops=7_046_430_720, bytes_accessed=11_000_000, transcendentals=5_505_024
        ),
    )(*[pltpu.with_memory_space_constraint(operand, pltpu.HBM) for operand in operands])
    query_grad, key_grad, value_grad, table_grad = result
    return (query_grad[None], key_grad[None], value_grad[None], table_grad)


def solution(mesh):
    rows = P("dp", "seq", None)
    return jax.shard_map(
        per_device,
        mesh=mesh,
        in_specs=(rows, rows, rows, rows, P("dp", None), P(), P("seq", None), P("seq", None)),
        out_specs=(rows, rows, rows, P("dp", None)),
        check_vma=False,
    )
```
